256 devices in a mesh: acq: 128 (over x, z, y), slab: 2 (over core).
Axes of the slice: x: 4, y: 4, z: 8, core: 2. Of those that a mesh axis runs over, the one named last changes fastest.
Arguments:
- slc_amplitude: float32 [256, 160, 1280], P('acq', None, 'slab'), may hold values from 0.3 to 3
- slc_phase: float32 [256, 160, 1280], P('acq', None, 'slab'), may hold values from -9.5 to 9.5
- pair_list: int32 [512, 2], replicated, may hold values from 0 to 255, as said below
- pair_owner: int32 [512], replicated, may hold values from 0 to 127, as said below
- tile_map: int32 [128], replicated, may hold values from 0 to 127, as said below
Outputs:
- interferograms: float32 [512, 2, 32, 256], P('acq', None, None, 'slab')
- linked_phases: float32 [256, 2, 32, 256], P('acq', None, None, 'slab')
- tile_quality: float32 [256, 2, 32], P('acq', 'slab')
The draws below stay inside these ranges and needn't reach their ends.
Inputs may be any that keep to these rules, and one draw needn't show every extreme that they name: `pair_list`: each row is (r, s) with r < s. One of the two acquisitions is held by the pair's owner and the other by the owner or by a device beside it along acq; every device but the first owns a pair whose other acquisition is held by the device before it, and every device but the last owns one whose other acquisition is held by the device after it. `pair_owner`: every device owns exactly 4 pairs. `tile_map`: every device owns at most 2 tiles, and some device owns exactly 2.
All inputs are finite; a program needn't handle non-finite values.
Results may differ from the reference program's by a relative error of at most 0.0001.
Values sent between devices are 32-bit elements; how exact they have to be, the bound alone decides.
A program may use at most 64 MiB of HBM per device.

```python
import math
import jax
import jax.numpy as jnp
from jax import lax

ACQ_DEV = 2
PAIR_DEV = 4
LOOK = 5
ITERS = 8
LCOLS = 32
ACQS = 256
PAIRS = 512
TILES = 128
TILE_CAP = 2
ROWS = 1280
COLS = 160
LROWS = 256
N_ACQ = 128
N_SLAB = 2


def pair_tables(key):
    key_one, key_two, key_three = jax.random.split(jax.random.fold_in(key, 7), 3)
    device_of = jnp.repeat(jnp.arange(N_ACQ, dtype=jnp.int32), PAIR_DEV)
    slot_of = jnp.tile(jnp.arange(PAIR_DEV, dtype=jnp.int32), N_ACQ)
    count_all = N_ACQ * PAIR_DEV
    local_acq = device_of * ACQ_DEV + jax.random.randint(key_one, (count_all,), 0, ACQ_DEV)
    lower = jnp.maximum(device_of * ACQ_DEV - ACQ_DEV, 0)
    upper = jnp.minimum(device_of * ACQ_DEV + 2 * ACQ_DEV, N_ACQ * ACQ_DEV)
    lower = jnp.where((slot_of == 1) & (device_of < N_ACQ - 1), (device_of + 1) * ACQ_DEV, lower)
    upper = jnp.where((slot_of == 0) & (device_of > 0), device_of * ACQ_DEV, upper)
    covers = ((local_acq >= lower) & (local_acq < upper)).astype(jnp.int32)
    picked = lower + jax.random.randint(key_two, (count_all,), 0, upper - lower - covers)
    partner = picked + (picked >= local_acq).astype(jnp.int32) * covers
    pairs = jnp.stack([jnp.minimum(local_acq, partner), jnp.maximum(local_acq, partner)], axis=1)
    shuffle = jax.random.permutation(key_three, count_all)
    return (pairs[shuffle].astype(jnp.int32), device_of[shuffle].astype(jnp.int32))


def draw_pair_list(key, part):
    return pair_tables(key)[0]


def draw_pair_owner(key, part):
    return pair_tables(key)[1]


def draw_tile_map(key, part):
    key_one, key_two, key_three = jax.random.split(jax.random.fold_in(key, 11), 3)
    shares = jax.random.randint(key_one, (N_ACQ // 2,), 0, TILE_CAP + 1).at[0].set(TILE_CAP)
    counts = jnp.stack([shares, TILE_CAP - shares], axis=1).reshape(N_ACQ)
    bounds = jnp.cumsum(counts)
    position = jnp.arange(TILES, dtype=jnp.int32)
    slot_group = jnp.sum((position[:, None] >= bounds[None, :]).astype(jnp.int32), axis=1)
    dev_order = jax.random.permutation(key_two, N_ACQ).astype(jnp.int32)
    owners = dev_order[slot_group]
    return owners[jax.random.permutation(key_three, TILES)].astype(jnp.int32)


def draw_slc_phase(key, part):
    key_one, key_two, key_three = jax.random.split(jax.random.fold_in(key, 13), 3)
    common_phase = jax.random.uniform(key_one, (1, COLS, ROWS), jnp.float32, -math.pi, math.pi)
    acq_drift = jax.random.uniform(key_two, (ACQS, 1, 1), jnp.float32, -math.pi, math.pi)
    speckle = jax.random.uniform(key_three, (ACQS, COLS, ROWS), jnp.float32, -2.0, 2.0)
    return (common_phase + acq_drift + speckle).astype(jnp.float32)


def steps_of(stream_key, extent, cuts, smallest, top_value):
    def one(axis_at, blocks):
        steps = jax.random.uniform(jax.random.fold_in(jax.random.fold_in(stream_key, 6), axis_at), (blocks,), jnp.float32, smallest / len(cuts), top_value / len(cuts))
        return jnp.repeat(jnp.exp(steps), extent[axis_at] // blocks).reshape((-1,) + (1,) * (len(extent) - axis_at - 1))

    level = one(*cuts[0])
    for cut in cuts[1:]:
        level = level * one(*cut)
    return level


def setup_inputs(seed: int = 0) -> dict:
    splits = jax.random.split(jax.random.key(seed), 6)
    slc_amplitude = jnp.clip(jnp.exp(math.log(3.0) - 2.3025851 * jax.random.uniform(splits[0], (ACQS, COLS, ROWS), jnp.float32) ** steps_of(splits[0], (ACQS, COLS, ROWS), ((0, 128), (2, 2)), -0.2, 0.2)), 0.3, 3.0)
    slc_phase = draw_slc_phase(jax.random.fold_in(splits[5], 71), 0)
    pair_list = draw_pair_list(jax.random.fold_in(splits[5], 71), 0)
    pair_owner = draw_pair_owner(jax.random.fold_in(splits[5], 71), 0)
    tile_map = draw_tile_map(jax.random.fold_in(splits[5], 71), 0)
    return dict(slc_amplitude=slc_amplitude, slc_phase=slc_phase, pair_list=pair_list, pair_owner=pair_owner, tile_map=tile_map)


def multilook(field):
    dims = field.shape
    return field.reshape(dims[:-2] + (dims[-2] // LOOK, LOOK, dims[-1] // LOOK, LOOK)).sum(axis=(-3, -1))

def form_pair(amplitude, phase, members):
    ref_amp = amplitude[members[0]]
    ref_phase = phase[members[0]]
    sec_amp = amplitude[members[1]]
    sec_phase = phase[members[1]]
    ref_real = ref_amp * jnp.cos(ref_phase)
    ref_imag = ref_amp * jnp.sin(ref_phase)
    sec_real = sec_amp * jnp.cos(sec_phase)
    sec_imag = sec_amp * jnp.sin(sec_phase)
    cross_real = multilook(ref_real * sec_real + ref_imag * sec_imag)
    cross_imag = multilook(ref_imag * sec_real - ref_real * sec_imag)
    ref_power = multilook(ref_real * ref_real + ref_imag * ref_imag)
    sec_power = multilook(sec_real * sec_real + sec_imag * sec_imag)
    norm_value = jnp.sqrt(ref_power * sec_power)
    return jnp.stack([cross_real / norm_value, cross_imag / norm_value])

def reference(slc_amplitude, slc_phase, pair_list, pair_owner, tile_map):
    owner_order = jnp.argsort(pair_owner, stable=True).astype(jnp.int32)
    slotted = pair_list[owner_order]
    interferograms = lax.map(lambda members: form_pair(slc_amplitude, slc_phase, members), slotted)
    pixel_count = LROWS * LCOLS
    coherence = interferograms.reshape(PAIRS, 2, pixel_count)
    coh_real = coherence[:, 0]
    coh_imag = coherence[:, 1]
    ref_index = slotted[:, 0]
    sec_index = slotted[:, 1]
    unit_ones = jnp.ones((PAIRS,), jnp.float32)
    degree = jax.ops.segment_sum(unit_ones, ref_index, num_segments=ACQS) + jax.ops.segment_sum(unit_ones, sec_index, num_segments=ACQS)
    vector = jnp.stack([jnp.ones((ACQS, pixel_count), jnp.float32), jnp.zeros((ACQS, pixel_count), jnp.float32)], axis=1)
    for iteration in range(ITERS):
        ref_vec = vector[ref_index]
        sec_vec = vector[sec_index]
        ref_term = jnp.stack([coh_real * sec_vec[:, 0] - coh_imag * sec_vec[:, 1], coh_real * sec_vec[:, 1] + coh_imag * sec_vec[:, 0]], axis=1)
        sec_term = jnp.stack([coh_real * ref_vec[:, 0] + coh_imag * ref_vec[:, 1], coh_real * ref_vec[:, 1] - coh_imag * ref_vec[:, 0]], axis=1)
        product = (1.0 + degree)[:, None, None] * vector
        product = product + jax.ops.segment_sum(ref_term, ref_index, num_segments=ACQS)
        product = product + jax.ops.segment_sum(sec_term, sec_index, num_segments=ACQS)
        vector = product * jnp.sqrt(ACQS / (lax.optimization_barrier(jnp.sum(product * product, axis=(0, 1))) + 1e-06))
    ref_vec = vector[ref_index]
    sec_vec = vector[sec_index]
    mixed_real = ref_vec[:, 0] * sec_vec[:, 0] + ref_vec[:, 1] * sec_vec[:, 1]
    mixed_imag = ref_vec[:, 0] * sec_vec[:, 1] - ref_vec[:, 1] * sec_vec[:, 0]
    quality = lax.optimization_barrier(jnp.sum(coh_real * mixed_real - coh_imag * mixed_imag, axis=0)) / PAIRS
    linked = vector.reshape(ACQS, 2, LCOLS, LROWS)
    devices_range = jnp.arange(N_ACQ, dtype=jnp.int32)
    tile_hits = (tile_map[:, None] == devices_range[None, :]).astype(jnp.int32)
    tile_rank = lax.optimization_barrier(jnp.sum(jnp.cumsum(tile_hits, axis=0) * tile_hits, axis=1)) - 1
    slot_key = (tile_map * TILE_CAP + tile_rank).astype(jnp.int32)
    per_row = quality.reshape(LCOLS, N_SLAB, TILES).transpose(2, 1, 0)
    tile_quality = jnp.zeros((N_ACQ * TILE_CAP, N_SLAB, LCOLS), jnp.float32).at[slot_key].set(per_row)
    return (interferograms, linked, tile_quality)
```

```python
from functools import partial

import jax
import jax.numpy as jnp
from jax import lax
from jax.experimental import pallas as pl
from jax.experimental.pallas import tpu as pltpu
from jax.sharding import PartitionSpec as P

MESH = pl.DeviceIdType.MESH
F32 = jnp.float32
BF16 = jnp.bfloat16
LOOK = 5
ITERS = 8
TILE_CAP = 2
EPS = 1e-06
HALO = 8
LANES = 128
SUB = 8
GROUP = SUB * LOOK


def sincos(x):
    turns = jnp.floor(x * 0.6366197723675814 + 0.5)
    r = ((x - turns * 1.5703125) - turns * 4.837512969970703e-4) - turns * 7.54978995489188e-8
    z = r * r
    s = ((-1.9515295891e-4 * z + 8.3321608736e-3) * z - 1.6666654611e-1) * z * r + r
    c = ((2.443315711809948e-5 * z - 1.388731625493765e-3) * z + 4.166664568298827e-2) * z * z
    c = c - 0.5 * z + 1.0
    quarter = turns.astype(jnp.int32)
    odd = (quarter & 1) == 1
    sin = jnp.where(odd, c, s)
    cos = jnp.where(odd, s, c)
    sin = jnp.where((quarter & 2) == 2, -sin, sin)
    cos = jnp.where(((quarter + 1) & 2) == 2, -cos, cos)
    return sin, cos


def total(x):
    return jnp.sum(jnp.sum(x, axis=1, keepdims=True), axis=0, keepdims=True)


def smallest(x):
    return jnp.min(jnp.min(x, axis=1, keepdims=True), axis=0, keepdims=True)


def kernel(
    tab_ref, amp_hbm, ph_hbm, ifg_ref, link_ref, qual_ref,
    amp, ph, smp, from_left, from_right, acc, win, gee, power, loc, emsg, ebuf, lmsg, lbuf,
    edge, vec, deg, umsg, ubuf, nmsg, nbuf, amsg, abuf,
    in_sem, s_send, s_recv, g_send, g_recv, e_send, h_send, e_recv, l_send, lh_send, l_recv,
    u_send, u_recv, n_send, n_recv, a_send, a_recv,
):
    devices = lax.axis_size("acq")
    columns = loc.shape[1]
    planes = devices // columns
    half = columns // 2
    rows_w = columns + 2 * HALO
    lane_tiles = smp.shape[2]
    pairs_total = 4 * devices
    acq_total = 2 * devices
    me = lax.axis_index("acq")
    plane = me // columns
    cs = lax.rem(me, columns)
    right = lax.rem(me + 1, devices)
    left = lax.rem(me + devices - 1, devices)
    above = lax.rem(plane + 1, planes)
    below = lax.rem(plane + planes - 1, planes)

    def remote(src, dst, send, recv, target):
        return pltpu.make_async_remote_copy(
            src_ref=src, dst_ref=dst, send_sem=send, recv_sem=recv,
            device_id={"acq": target}, device_id_type=MESH,
        )

    def await_bytes(ref, sem):
        pltpu.make_async_copy(ref, ref, sem).wait()

    order = (0, 2, 1, 3)
    for g in order:
        for a, (src, dst) in enumerate(((amp_hbm, amp), (ph_hbm, ph))):
            cut = pl.ds(g * GROUP, GROUP)
            pltpu.make_async_copy(src.at[:, cut, :], dst.at[:, cut, :], in_sem.at[a, g]).start()

    barrier = pltpu.get_barrier_semaphore()

    def tell(target):
        pl.semaphore_signal(barrier, inc=1, device_id={"acq": target}, device_id_type=MESH)

    tell(left)
    tell(right)

    @pl.loop(1, columns)
    def _(i):
        tell(plane * columns + lax.rem(cs + i, columns))

    for i in range(1, planes):
        tell(lax.rem(plane + i, planes) * columns + cs)

    @pl.loop(0, HALO + 1)
    def _(i):
        tell(above * columns + i)

    @pl.loop(0, HALO)
    def _(i):
        tell(below * columns + columns - HALO + i)

    def form_samples(g):
        for a, (src, dst) in enumerate(((amp_hbm, amp), (ph_hbm, ph))):
            cut = pl.ds(g * GROUP, GROUP)
            pltpu.make_async_copy(src.at[:, cut, :], dst.at[:, cut, :], in_sem.at[a, g]).wait()

        @pl.loop(0, LOOK)
        def _(i):
            cut = pl.ds(pl.multiple_of(g * GROUP + i * SUB, SUB), SUB)
            here = pl.ds(pl.multiple_of(i * SUB, SUB), SUB)
            for a in range(2):
                size = amp[a, cut, :]
                sin, cos = sincos(ph[a, cut, :])
                real, imag = size * cos, size * sin
                for lt in range(lane_tiles):
                    lanes = slice(lt * LANES, (lt + 1) * LANES)
                    smp[g, 2 * a, lt, here, :] = real[:, lanes]
                    smp[g, 2 * a + 1, lt, here, :] = imag[:, lanes]

    def sample_copy(side, k):
        if side == 0:
            return remote(smp.at[k], from_left.at[k], s_send.at[0, k], s_recv.at[0, k], right)
        return remote(smp.at[2 + k], from_right.at[k], s_send.at[1, k], s_recv.at[1, k], left)

    form_samples(0)
    form_samples(2)
    in_halo = jnp.logical_or(cs <= HALO, cs >= columns - HALO).astype(jnp.int32)
    pl.semaphore_wait(barrier, 2 + (columns - 1) + (planes - 1) + columns * in_halo)
    sample_copy(0, 0).start()
    sample_copy(1, 0).start()
    form_samples(1)
    form_samples(3)
    sample_copy(0, 1).start()
    sample_copy(1, 1).start()

    raw = lax.broadcasted_iota(jnp.int32, win.shape, 0)
    low = lax.broadcasted_iota(jnp.int32, win.shape, 1) * LOOK
    win[...] = jnp.where((raw >= low) & (raw < low + LOOK), 1.0, 0.0).astype(BF16)

    def look(count):
        x = acc[0:count, :]
        high = x.astype(BF16)
        rest = (x - high.astype(F32)).astype(BF16)
        return jnp.dot(high, win[...], preferred_element_type=F32) + jnp.dot(
            rest, win[...], preferred_element_type=F32
        )

    key = tab_ref[0:4, :] * 256 + tab_ref[4:8, :]
    base = 2 * me

    def key_of(i, j):
        return (base + i) * 256 + base + j

    codes = [[key_of(i - 2, j) for i in range(2) for j in range(2)],
             [key_of(i, j + 2) for i in range(2) for j in range(2)]]
    code_own = key_of(0, 1)

    def count_of(code):
        return total(jnp.where(key == code, 1.0, 0.0))

    weight = [[count_of(c) for c in side] for side in codes]
    weight_own = count_of(code_own)

    index = (
        lax.broadcasted_iota(jnp.int32, (4, LANES), 0) * LANES
        + lax.broadcasted_iota(jnp.int32, (4, LANES), 1)
    ).astype(F32)
    key_f = key.astype(F32)
    big = 1e6
    left_over = jnp.where(tab_ref[8:12, :] == me, index, big)
    slot_key = []
    for _ in range(4):
        first = smallest(left_over)
        hit = index == first
        slot_key.append(total(jnp.where(hit, key_f, 0.0)).astype(jnp.int32))
        left_over = jnp.where(hit, big, left_over)

    ones = jnp.ones((LANES, LANES), BF16)
    window_dev = lax.rem(
        lax.broadcasted_iota(jnp.int32, (rows_w, LANES), 0)
        + (plane * columns + devices - HALO),
        devices,
    )
    for i in range(2):
        acq = 2 * window_dev + i
        hits = jnp.zeros((rows_w, LANES), F32)
        for q in range(8):
            hits = hits + jnp.where(acq == tab_ref[q : q + 1, :], 1.0, 0.0)
        deg[i] = 1.0 + jnp.dot(hits.astype(BF16), ones, preferred_element_type=F32)

    @pl.loop(0, 4)
    def _(g):
        @pl.loop(0, lane_tiles)
        def _(lt):
            lanes = pl.ds(pl.multiple_of(lt * LANES, LANES), LANES)
            sums = [jnp.zeros((SUB, LANES), F32) for _ in range(4)]
            for kk in range(LOOK):
                x = [smp[g, f, lt, pl.ds(kk, SUB, stride=LOOK), :] for f in range(4)]
                sums[0] = sums[0] + (x[0] * x[0] + x[1] * x[1])
                sums[1] = sums[1] + (x[2] * x[2] + x[3] * x[3])
                sums[2] = sums[2] + (x[0] * x[2] + x[1] * x[3])
                sums[3] = sums[3] + (x[1] * x[2] - x[0] * x[3])
            for f in range(4):
                acc[f * SUB : (f + 1) * SUB, lanes] = sums[f]

        out = look(4 * SUB)
        cut = pl.ds(pl.multiple_of(g * SUB, SUB), SUB)
        power_ref, power_sec = out[0:SUB], out[SUB : 2 * SUB]
        power[0, cut, :] = power_ref
        power[1, cut, :] = power_sec
        scale = 1.0 / jnp.sqrt(power_ref * power_sec)
        loc[0, cut, :] = out[2 * SUB : 3 * SUB] * scale
        loc[1, cut, :] = out[3 * SUB : 4 * SUB] * scale

    for f in range(2):
        lmsg[:, f, :] = loc[f] * weight_own

    here = HALO + cs

    @pl.loop(1, columns)
    def _(i):
        c = lax.rem(cs + i, columns)
        remote(lmsg.at[c], lbuf.at[here], l_send, l_recv, plane * columns + c).start()

    @pl.when(cs < HALO)
    def _():
        @pl.loop(0, columns)
        def _(i):
            c = lax.rem(cs + i, columns)
            remote(
                lmsg.at[c], lbuf.at[columns + HALO + cs], lh_send, l_recv, below * columns + c
            ).start()

    @pl.when(cs >= columns - HALO)
    def _():
        @pl.loop(0, columns)
        def _(i):
            c = lax.rem(cs + i, columns)
            remote(
                lmsg.at[c], lbuf.at[cs - (columns - HALO)], lh_send, l_recv, above * columns + c
            ).start()

    lbuf[here] = lmsg[cs]

    vec[...] = jnp.zeros_like(vec)
    vec[0, 0] = jnp.ones(vec.shape[2:], F32)
    vec[0, 2] = jnp.ones(vec.shape[2:], F32)
    for f in range(8):
        edge[f, 0:SUB, :] = jnp.zeros((SUB, LANES), F32)

    def gee_copy(side, k):
        if side == 0:
            part = gee.at[0, :, pl.ds(SUB * k, SUB), :]
            return remote(
                part, gee.at[1, :, pl.ds(SUB * k, SUB), :], g_send.at[0, k], g_recv.at[0, k], left
            )
        part = gee.at[1, :, pl.ds(half + SUB * k, SUB), :]
        return remote(
            part, gee.at[0, :, pl.ds(half + SUB * k, SUB), :],
            g_send.at[1, k], g_recv.at[1, k], right,
        )

    def slot_rows(slot):
        return pl.ds(pl.multiple_of(SUB * slot, SUB), SUB)

    for k in range(2):
        for side in range(2):
            sample_copy(side, k).wait_recv()
            other = (from_left, from_right)[side]
            first_col = side * half + k * SUB

            @pl.loop(0, lane_tiles)
            def _(lt):
                lanes = pl.ds(pl.multiple_of(lt * LANES, LANES), LANES)
                sums = [jnp.zeros((SUB, LANES), F32) for _ in range(10)]
                for kk in range(LOOK):
                    cut = pl.ds(kk, SUB, stride=LOOK)
                    near = [smp[2 * side + k, f, lt, cut, :] for f in range(4)]
                    far = [other[k, f, lt, cut, :] for f in range(4)]
                    ref, sec = (far, near) if side == 0 else (near, far)
                    for i in range(2):
                        for j in range(2):
                            f = (2 * i + j) * 2
                            sums[f] = sums[f] + (
                                ref[2 * i] * sec[2 * j] + ref[2 * i + 1] * sec[2 * j + 1]
                            )
                            sums[f + 1] = sums[f + 1] + (
                                ref[2 * i + 1] * sec[2 * j] - ref[2 * i] * sec[2 * j + 1]
                            )
                        sums[8 + i] = sums[8 + i] + (
                            far[2 * i] * far[2 * i] + far[2 * i + 1] * far[2 * i + 1]
                        )
                for f in range(10):
                    acc[f * SUB : (f + 1) * SUB, lanes] = sums[f]

            out = look(10 * SUB)
            for i in range(2):
                for j in range(2):
                    mine, theirs = (j, i) if side == 0 else (i, j)
                    scale = 1.0 / jnp.sqrt(
                        power[mine, first_col : first_col + SUB, :]
                        * out[(8 + theirs) * SUB : (9 + theirs) * SUB]
                    )
                    for part in range(2):
                        f = (2 * i + j) * 2 + part
                        value = out[f * SUB : (f + 1) * SUB] * scale
                        gee[side, f, first_col : first_col + SUB, :] = value
                        emsg[pl.ds(SUB * first_col + f, SUB, stride=SUB), :] = (
                            value * weight[side][2 * i + j]
                        )

            edge_at = cs - 1 if side == 0 else cs

            @pl.loop(0, SUB)
            def _(i):
                c = first_col + lax.rem(cs + i, SUB)
                src = emsg.at[slot_rows(c), :]

                @pl.when(c != cs)
                def _():
                    remote(
                        src, ebuf.at[slot_rows(HALO + edge_at), :], e_send, e_recv,
                        plane * columns + c,
                    ).start()

                @pl.when(edge_at < HALO)
                def _():
                    remote(
                        src, ebuf.at[slot_rows(columns + HALO + edge_at), :], h_send, e_recv,
                        below * columns + c,
                    ).start()

                @pl.when(edge_at >= columns - HALO)
                def _():
                    remote(
                        src, ebuf.at[slot_rows(edge_at - (columns - HALO)), :], h_send, e_recv,
                        above * columns + c,
                    ).start()

        for side in range(2):
            gee_copy(side, k).start()

    shift = (cs < half).astype(jnp.int32)
    ebuf[slot_rows(here - shift), :] = emsg[slot_rows(cs), :]

    await_bytes(lbuf.at[pl.ds(0, rows_w - 1)], l_recv)
    await_bytes(ebuf.at[pl.ds(0, (rows_w - 1) * SUB), :], e_recv)
    for f in range(8):
        for t in range(rows_w // SUB):
            edge[f, SUB * (t + 1) : SUB * (t + 2), :] = ebuf[
                pl.ds(f + SUB * SUB * t, SUB, stride=SUB), :
            ]
    loc_w = [lbuf[:, f, :] for f in range(2)]
    for f in range(2):
        edge[8 + f, SUB : SUB + rows_w, :] = loc_w[f]

    def step(t, kappa):
        now = lax.rem(t, 2)
        size = jnp.zeros((SUB, LANES), F32)
        for w in range(rows_w // SUB):
            cut = slice(SUB * w, SUB * (w + 1))
            mid = slice(SUB * (w + 1), SUB * (w + 2))
            low = slice(SUB * (w + 1) - 1, SUB * (w + 2) - 1)
            high = slice(SUB * (w + 1) + 1, SUB * (w + 2) + 1)
            u = [vec[now, f, mid, :] for f in range(4)]
            u_low = [vec[now, f, low, :] for f in range(4)]
            u_high = [vec[now, f, high, :] for f in range(4)]
            lr, li = edge[8, mid, :], edge[9, mid, :]
            for a in range(2):
                d = deg[a, cut, :]
                o = 1 - a
                sign = 1.0 if a == 0 else -1.0
                re = d * u[2 * a] + lr * u[2 * o] - sign * (li * u[2 * o + 1])
                im = d * u[2 * a + 1] + lr * u[2 * o + 1] + sign * (li * u[2 * o])
                for b in range(2):
                    f = (2 * a + b) * 2
                    gr, gi = edge[f, mid, :], edge[f + 1, mid, :]
                    re = re + (gr * u_high[2 * b] - gi * u_high[2 * b + 1])
                    im = im + (gr * u_high[2 * b + 1] + gi * u_high[2 * b])
                    f = (2 * b + a) * 2
                    gr, gi = edge[f, low, :], edge[f + 1, low, :]
                    re = re + (gr * u_low[2 * b] + gi * u_low[2 * b + 1])
                    im = im + (gr * u_low[2 * b + 1] - gi * u_low[2 * b])
                vec[1 - now, 2 * a, mid, :] = re
                vec[1 - now, 2 * a + 1, mid, :] = im
                if HALO // SUB <= w < (HALO + columns) // SUB:
                    size = size + (re * re + im * im)
        return (jnp.sum(size, axis=0, keepdims=True) + EPS * kappa) / acq_total

    kappa = lax.fori_loop(0, ITERS, step, jnp.full((1, LANES), 1.0 / planes, F32))
    last = ITERS % 2
    nmsg[0:1, :] = kappa

    own = slice(SUB + HALO, SUB + HALO + columns)
    for f in range(4):
        umsg[:, f, :] = vec[last, f, own, :]

    @pl.loop(1, columns)
    def _(i):
        c = lax.rem(cs + i, columns)
        remote(umsg.at[c], ubuf.at[cs], u_send, u_recv, plane * columns + c).start()

    qual = jnp.zeros((SUB, LANES), F32)
    for w in range(HALO // SUB, (HALO + columns) // SUB):
        mid = slice(SUB * (w + 1), SUB * (w + 2))
        high = slice(SUB * (w + 1) + 1, SUB * (w + 2) + 1)
        u = [vec[last, f, mid, :] for f in range(4)]
        u_high = [vec[last, f, high, :] for f in range(4)]
        qual = qual + edge[8, mid, :] * (u[0] * u[2] + u[1] * u[3])
        qual = qual - edge[9, mid, :] * (u[0] * u[3] - u[1] * u[2])
        for a in range(2):
            for b in range(2):
                f = (2 * a + b) * 2
                ur, ui = u[2 * a], u[2 * a + 1]
                vr, vi = u_high[2 * b], u_high[2 * b + 1]
                qual = qual + edge[f, mid, :] * (ur * vr + ui * vi)
                qual = qual - edge[f + 1, mid, :] * (ur * vi - ui * vr)
    nmsg[1:2, :] = jnp.sum(qual, axis=0, keepdims=True)
    for i in range(1, planes):
        target = lax.rem(plane + i, planes) * columns + cs
        remote(nmsg, nbuf.at[plane], n_send, n_recv, target).start()
    nbuf[plane] = nmsg[...]
    ubuf[cs] = umsg[cs]

    for side in range(2):
        for k in range(2):
            gee_copy(side, k).wait_recv()
    for slot in range(4):
        hit_own = slot_key[slot] == code_own
        hits = [[slot_key[slot] == c for c in side] for side in codes]

        @pl.loop(0, columns // SUB)
        def _(g):
            cut = pl.ds(pl.multiple_of(g * SUB, SUB), SUB)
            for part in range(2):
                value = jnp.where(hit_own, loc[part, cut, :], 0.0)
                for side in range(2):
                    for c in range(4):
                        value = jnp.where(hits[side][c], gee[side, 2 * c + part, cut, :], value)
                ifg_ref[slot, part, cut, :] = value

    await_bytes(nbuf.at[pl.ds(0, planes - 1)], n_recv)
    both = nbuf[0]
    for i in range(1, planes):
        both = both + nbuf[i]
    kappa, qual = both[0:1, :], both[1:2, :]
    amsg[0:1, :] = 1.0 / jnp.sqrt(kappa)
    amsg[1:2, :] = qual / (kappa * pairs_total)

    @pl.loop(1, columns)
    def _(i):
        c = lax.rem(cs + i, columns)
        remote(amsg, abuf.at[cs], a_send, a_recv, plane * columns + c).start()

    abuf[cs] = amsg[...]

    tile = lax.broadcasted_iota(jnp.int32, (1, LANES), 1).astype(F32)
    free = jnp.where(tab_ref[12:13, :] == me, tile, big)
    picks = []
    for _ in range(TILE_CAP):
        first = jnp.min(free, axis=1, keepdims=True)
        hit = tile == first
        picks.append(jnp.where(hit, 1.0, 0.0))
        free = jnp.where(hit, big, free)

    await_bytes(ubuf.at[pl.ds(0, columns - 1)], u_recv)
    await_bytes(abuf.at[pl.ds(0, columns - 1)], a_recv)
    alpha = abuf[:, 0, :]
    for a in range(2):
        for part in range(2):
            link_ref[a, part] = ubuf[:, 2 * a + part, :] * alpha
    quality = abuf[:, 1, :]
    pick = jnp.concatenate(picks + [jnp.zeros((SUB - TILE_CAP, LANES), F32)], axis=0)
    chosen = lax.dot_general(
        pick, quality, (((1,), (1,)), ((), ())),
        precision=lax.Precision.HIGHEST, preferred_element_type=F32,
    )
    for a in range(TILE_CAP):
        qual_ref[a] = chosen[a : a + 1, :]

    for side in range(2):
        for k in range(2):
            sample_copy(side, k).wait_send()
            gee_copy(side, k).wait_send()
    await_bytes(lmsg.at[pl.ds(0, columns - 1)], l_send)
    await_bytes(emsg.at[pl.ds(0, (columns - 1) * SUB), :], e_send)
    await_bytes(ubuf.at[pl.ds(0, columns - 1)], u_send)
    await_bytes(abuf.at[pl.ds(0, columns - 1)], a_send)
    await_bytes(nbuf.at[pl.ds(0, planes - 1)], n_send)

    @pl.when(jnp.logical_or(cs < HALO, cs >= columns - HALO))
    def _():
        await_bytes(lmsg, lh_send)

    for side in range(2):
        edge_at = cs - 1 if side == 0 else cs

        @pl.when(jnp.logical_or(edge_at < HALO, edge_at >= columns - HALO))
        def _():
            await_bytes(emsg.at[pl.ds(0, half * SUB), :], h_send)


def per_device(slc_amplitude, slc_phase, pair_list, pair_owner, tile_map):
    columns = slc_amplitude.shape[1] // LOOK
    raw = slc_amplitude.shape[2]
    table = jnp.concatenate([pair_list.T.reshape(-1), pair_owner, tile_map]).reshape(-1, LANES)
    rows_w = columns + 2 * HALO
    dma = pltpu.SemaphoreType.DMA
    vmem = pl.BlockSpec(memory_space=pltpu.VMEM)
    return tuple(
        pl.pallas_call(
            kernel,
            name="phase_linking",
            out_shape=(
                jax.ShapeDtypeStruct((4, 2, columns, LANES), F32),
                jax.ShapeDtypeStruct((2, 2, columns, LANES), F32),
                jax.ShapeDtypeStruct((TILE_CAP, 1, columns), F32),
            ),
            in_specs=[vmem, pl.BlockSpec(memory_space=pl.ANY), pl.BlockSpec(memory_space=pl.ANY)],
            out_specs=(vmem, vmem, vmem),
            scratch_shapes=[
                pltpu.VMEM(slc_amplitude.shape, F32),
                pltpu.VMEM(slc_amplitude.shape, F32),
                pltpu.VMEM((4, 4, raw // LANES, GROUP, LANES), F32),
                pltpu.VMEM((2, 4, raw // LANES, GROUP, LANES), F32),
                pltpu.VMEM((2, 4, raw // LANES, GROUP, LANES), F32),
                pltpu.VMEM((10 * SUB, raw), F32),
                pltpu.VMEM((raw, LANES), BF16),
                pltpu.VMEM((2, 8, columns, LANES), F32),
                pltpu.VMEM((2, columns, LANES), F32),
                pltpu.VMEM((2, columns, LANES), F32),
                pltpu.VMEM((columns * SUB, LANES), F32),
                pltpu.VMEM((rows_w * SUB, LANES), F32),
                pltpu.VMEM((columns, 2, LANES), F32),
                pltpu.VMEM((rows_w, 2, LANES), F32),
                pltpu.VMEM((10, rows_w + 2 * SUB, LANES), F32),
                pltpu.VMEM((2, 4, rows_w + 2 * SUB, LANES), F32),
                pltpu.VMEM((2, rows_w, LANES), F32),
                pltpu.VMEM((columns, 4, LANES), F32),
                pltpu.VMEM((columns, 4, LANES), F32),
                pltpu.VMEM((2, LANES), F32),
                pltpu.VMEM((4, 2, LANES), F32),
                pltpu.VMEM((2, LANES), F32),
                pltpu.VMEM((columns, 2, LANES), F32),
                dma((2, 4)), dma((2, 2)), dma((2, 2)), dma((2, 2)), dma((2, 2)),
                dma, dma, dma, dma, dma, dma, dma, dma, dma, dma, dma, dma,
            ],
            compiler_params=pltpu.CompilerParams(
                collective_id=0, has_side_effects=True, vmem_limit_bytes=40 * 2**20
            ),
        )(table, slc_amplitude, slc_phase)
    )


def solution(mesh):
    in_specs = (P("acq", None, "slab"), P("acq", None, "slab"), P(), P(), P())
    out_specs = (P("acq", None, None, "slab"), P("acq", None, None, "slab"), P("acq", "slab", None))
    return jax.shard_map(
        per_device, mesh=mesh, in_specs=in_specs, out_specs=out_specs, check_vma=False
    )
```

```python
from functools import partial

import jax
import jax.numpy as jnp
from jax import lax
from jax.experimental import pallas as pl
from jax.experimental.pallas import tpu as pltpu
from jax.sharding import PartitionSpec as P

MESH = pl.DeviceIdType.MESH
F32 = jnp.float32
BF16 = jnp.bfloat16
LOOK = 5
ITERS = 8
TILE_CAP = 2
EPS = 1e-06
HALO = 8
LANES = 128
SUB = 8
GROUP = SUB * LOOK


def sincos(x):
    turns = jnp.floor(x * 0.6366197723675814 + 0.5)
    r = ((x - turns * 1.5703125) - turns * 4.837512969970703e-4) - turns * 7.54978995489188e-8
    z = r * r
    s = ((-1.9515295891e-4 * z + 8.3321608736e-3) * z - 1.6666654611e-1) * z * r + r
    c = ((2.443315711809948e-5 * z - 1.388731625493765e-3) * z + 4.166664568298827e-2) * z * z
    c = c - 0.5 * z + 1.0
    quarter = turns.astype(jnp.int32)
    odd = (quarter & 1) == 1
    sin = jnp.where(odd, c, s)
    cos = jnp.where(odd, s, c)
    sin = jnp.where((quarter & 2) == 2, -sin, sin)
    cos = jnp.where(((quarter + 1) & 2) == 2, -cos, cos)
    return sin, cos


def total(x):
    return jnp.sum(jnp.sum(x, axis=1, keepdims=True), axis=0, keepdims=True)


def smallest(x):
    return jnp.min(jnp.min(x, axis=1, keepdims=True), axis=0, keepdims=True)


def kernel(
    amp_hbm, ph_hbm, pair_hbm, owner_hbm, tile_hbm, ifg_ref, link_ref, qual_ref,
    amp, ph, pair_tab, owner_tab, tile_tab, smp, from_left, from_right, acc, win, gee, power, loc, emsg, ebuf, lmsg, lbuf,
    edge, vec, deg, umsg, ubuf, nmsg, nbuf, amsg, abuf,
    in_sem, tab_sem, s_send, s_recv, g_send, g_recv, e_send, h_send, e_recv, l_send, lh_send, l_recv,
    u_send, u_recv, n_send, n_recv, a_send, a_recv,
):
    devices = lax.axis_size("acq")
    columns = loc.shape[1]
    planes = devices // columns
    half = columns // 2
    rows_w = columns + 2 * HALO
    lane_tiles = smp.shape[2]
    pairs_total = 4 * devices
    acq_total = 2 * devices
    me = lax.axis_index("acq")
    plane = me // columns
    cs = lax.rem(me, columns)
    right = lax.rem(me + 1, devices)
    left = lax.rem(me + devices - 1, devices)
    above = lax.rem(plane + 1, planes)
    below = lax.rem(plane + planes - 1, planes)

    def remote(src, dst, send, recv, target):
        return pltpu.make_async_remote_copy(
            src_ref=src, dst_ref=dst, send_sem=send, recv_sem=recv,
            device_id={"acq": target}, device_id_type=MESH,
        )

    def await_bytes(ref, sem):
        pltpu.make_async_copy(ref, ref, sem).wait()

    order = (0, 2, 1, 3)
    for g in order:
        for a, (src, dst) in enumerate(((amp_hbm, amp), (ph_hbm, ph))):
            cut = pl.ds(g * GROUP, GROUP)
            pltpu.make_async_copy(src.at[:, cut, :], dst.at[:, cut, :], in_sem.at[a, g]).start()

    tables = ((pair_hbm, pair_tab), (owner_hbm, owner_tab), (tile_hbm, tile_tab))
    for i, (src, dst) in enumerate(tables):
        pltpu.make_async_copy(src, dst, tab_sem.at[i]).start()

    barrier = pltpu.get_barrier_semaphore()

    def tell(target):
        pl.semaphore_signal(barrier, inc=1, device_id={"acq": target}, device_id_type=MESH)

    tell(left)
    tell(right)

    @pl.loop(1, columns)
    def _(i):
        tell(plane * columns + lax.rem(cs + i, columns))

    for i in range(1, planes):
        tell(lax.rem(plane + i, planes) * columns + cs)

    @pl.loop(0, HALO + 1)
    def _(i):
        tell(above * columns + i)

    @pl.loop(0, HALO)
    def _(i):
        tell(below * columns + columns - HALO + i)

    def form_samples(g):
        for a, (src, dst) in enumerate(((amp_hbm, amp), (ph_hbm, ph))):
            cut = pl.ds(g * GROUP, GROUP)
            pltpu.make_async_copy(src.at[:, cut, :], dst.at[:, cut, :], in_sem.at[a, g]).wait()

        @pl.loop(0, LOOK)
        def _(i):
            cut = pl.ds(pl.multiple_of(g * GROUP + i * SUB, SUB), SUB)
            here = pl.ds(pl.multiple_of(i * SUB, SUB), SUB)
            for a in range(2):
                size = amp[a, cut, :]
                sin, cos = sincos(ph[a, cut, :])
                real, imag = size * cos, size * sin
                for lt in range(lane_tiles):
                    lanes = slice(lt * LANES, (lt + 1) * LANES)
                    smp[g, 2 * a, lt, here, :] = real[:, lanes]
                    smp[g, 2 * a + 1, lt, here, :] = imag[:, lanes]

    def sample_copy(side, k):
        if side == 0:
            return remote(smp.at[k], from_left.at[k], s_send.at[0, k], s_recv.at[0, k], right)
        return remote(smp.at[2 + k], from_right.at[k], s_send.at[1, k], s_recv.at[1, k], left)

    form_samples(0)
    form_samples(2)
    in_halo = jnp.logical_or(cs <= HALO, cs >= columns - HALO).astype(jnp.int32)
    pl.semaphore_wait(barrier, 2 + (columns - 1) + (planes - 1) + columns * in_halo)
    sample_copy(0, 0).start()
    sample_copy(1, 0).start()
    form_samples(1)
    form_samples(3)
    sample_copy(0, 1).start()
    sample_copy(1, 1).start()

    raw = lax.broadcasted_iota(jnp.int32, win.shape, 0)
    low = lax.broadcasted_iota(jnp.int32, win.shape, 1) * LOOK
    win[...] = jnp.where((raw >= low) & (raw < low + LOOK), 1.0, 0.0).astype(BF16)

    def look(count):
        x = acc[0:count, :]
        high = x.astype(BF16)
        rest = (x - high.astype(F32)).astype(BF16)
        return jnp.dot(high, win[...], preferred_element_type=F32) + jnp.dot(
            rest, win[...], preferred_element_type=F32
        )

    for i, (src, dst) in enumerate(tables):
        pltpu.make_async_copy(src, dst, tab_sem.at[i]).wait()
    pair_ref, pair_sec = pair_tab[:, 0, :], pair_tab[:, 1, :]
    key = pair_ref * 256 + pair_sec
    base = 2 * me

    def key_of(i, j):
        return (base + i) * 256 + base + j

    codes = [[key_of(i - 2, j) for i in range(2) for j in range(2)],
             [key_of(i, j + 2) for i in range(2) for j in range(2)]]
    code_own = key_of(0, 1)

    def count_of(code):
        return total(jnp.where(key == code, 1.0, 0.0))

    weight = [[count_of(c) for c in side] for side in codes]
    weight_own = count_of(code_own)

    index = (
        lax.broadcasted_iota(jnp.int32, (4, LANES), 0) * LANES
        + lax.broadcasted_iota(jnp.int32, (4, LANES), 1)
    ).astype(F32)
    key_f = key.astype(F32)
    big = 1e6
    left_over = jnp.where(owner_tab[...] == me, index, big)
    slot_key = []
    for _ in range(4):
        first = smallest(left_over)
        hit = index == first
        slot_key.append(total(jnp.where(hit, key_f, 0.0)).astype(jnp.int32))
        left_over = jnp.where(hit, big, left_over)

    ones = jnp.ones((LANES, LANES), BF16)
    window_dev = lax.rem(
        lax.broadcasted_iota(jnp.int32, (rows_w, LANES), 0)
        + (plane * columns + devices - HALO),
        devices,
    )
    for i in range(2):
        acq = 2 * window_dev + i
        hits = jnp.zeros((rows_w, LANES), F32)
        for member in (pair_ref, pair_sec):
            for q in range(4):
                hits = hits + jnp.where(acq == member[q : q + 1, :], 1.0, 0.0)
        deg[i] = 1.0 + jnp.dot(hits.astype(BF16), ones, preferred_element_type=F32)

    @pl.loop(0, 4)
    def _(g):
        @pl.loop(0, lane_tiles)
        def _(lt):
            lanes = pl.ds(pl.multiple_of(lt * LANES, LANES), LANES)
            sums = [jnp.zeros((SUB, LANES), F32) for _ in range(4)]
            for kk in range(LOOK):
                x = [smp[g, f, lt, pl.ds(kk, SUB, stride=LOOK), :] for f in range(4)]
                sums[0] = sums[0] + (x[0] * x[0] + x[1] * x[1])
                sums[1] = sums[1] + (x[2] * x[2] + x[3] * x[3])
                sums[2] = sums[2] + (x[0] * x[2] + x[1] * x[3])
                sums[3] = sums[3] + (x[1] * x[2] - x[0] * x[3])
            for f in range(4):
                acc[f * SUB : (f + 1) * SUB, lanes] = sums[f]

        out = look(4 * SUB)
        cut = pl.ds(pl.multiple_of(g * SUB, SUB), SUB)
        power_ref, power_sec = out[0:SUB], out[SUB : 2 * SUB]
        power[0, cut, :] = power_ref
        power[1, cut, :] = power_sec
        scale = 1.0 / jnp.sqrt(power_ref * power_sec)
        loc[0, cut, :] = out[2 * SUB : 3 * SUB] * scale
        loc[1, cut, :] = out[3 * SUB : 4 * SUB] * scale

    for f in range(2):
        lmsg[:, f, :] = loc[f] * weight_own

    here = HALO + cs

    @pl.loop(1, columns)
    def _(i):
        c = lax.rem(cs + i, columns)
        remote(lmsg.at[c], lbuf.at[here], l_send, l_recv, plane * columns + c).start()

    @pl.when(cs < HALO)
    def _():
        @pl.loop(0, columns)
        def _(i):
            c = lax.rem(cs + i, columns)
            remote(
                lmsg.at[c], lbuf.at[columns + HALO + cs], lh_send, l_recv, below * columns + c
            ).start()

    @pl.when(cs >= columns - HALO)
    def _():
        @pl.loop(0, columns)
        def _(i):
            c = lax.rem(cs + i, columns)
            remote(
                lmsg.at[c], lbuf.at[cs - (columns - HALO)], lh_send, l_recv, above * columns + c
            ).start()

    lbuf[here] = lmsg[cs]

    vec[...] = jnp.zeros_like(vec)
    vec[0, 0] = jnp.ones(vec.shape[2:], F32)
    vec[0, 2] = jnp.ones(vec.shape[2:], F32)
    for f in range(8):
        edge[f, 0:SUB, :] = jnp.zeros((SUB, LANES), F32)

    def gee_copy(side, k):
        if side == 0:
            part = gee.at[0, :, pl.ds(SUB * k, SUB), :]
            return remote(
                part, gee.at[1, :, pl.ds(SUB * k, SUB), :], g_send.at[0, k], g_recv.at[0, k], left
            )
        part = gee.at[1, :, pl.ds(half + SUB * k, SUB), :]
        return remote(
            part, gee.at[0, :, pl.ds(half + SUB * k, SUB), :],
            g_send.at[1, k], g_recv.at[1, k], right,
        )

    def slot_rows(slot):
        return pl.ds(pl.multiple_of(SUB * slot, SUB), SUB)

    for k in range(2):
        for side in range(2):
            sample_copy(side, k).wait_recv()
            other = (from_left, from_right)[side]
            first_col = side * half + k * SUB

            @pl.loop(0, lane_tiles)
            def _(lt):
                lanes = pl.ds(pl.multiple_of(lt * LANES, LANES), LANES)
                sums = [jnp.zeros((SUB, LANES), F32) for _ in range(10)]
                for kk in range(LOOK):
                    cut = pl.ds(kk, SUB, stride=LOOK)
                    near = [smp[2 * side + k, f, lt, cut, :] for f in range(4)]
                    far = [other[k, f, lt, cut, :] for f in range(4)]
                    ref, sec = (far, near) if side == 0 else (near, far)
                    for i in range(2):
                        for j in range(2):
                            f = (2 * i + j) * 2
                            sums[f] = sums[f] + (
                                ref[2 * i] * sec[2 * j] + ref[2 * i + 1] * sec[2 * j + 1]
                            )
                            sums[f + 1] = sums[f + 1] + (
                                ref[2 * i + 1] * sec[2 * j] - ref[2 * i] * sec[2 * j + 1]
                            )
                        sums[8 + i] = sums[8 + i] + (
                            far[2 * i] * far[2 * i] + far[2 * i + 1] * far[2 * i + 1]
                        )
                for f in range(10):
                    acc[f * SUB : (f + 1) * SUB, lanes] = sums[f]

            out = look(10 * SUB)
            for i in range(2):
                for j in range(2):
                    mine, theirs = (j, i) if side == 0 else (i, j)
                    scale = 1.0 / jnp.sqrt(
                        power[mine, first_col : first_col + SUB, :]
                        * out[(8 + theirs) * SUB : (9 + theirs) * SUB]
                    )
                    for part in range(2):
                        f = (2 * i + j) * 2 + part
                        value = out[f * SUB : (f + 1) * SUB] * scale
                        gee[side, f, first_col : first_col + SUB, :] = value
                        emsg[pl.ds(SUB * first_col + f, SUB, stride=SUB), :] = (
                            value * weight[side][2 * i + j]
                        )

            edge_at = cs - 1 if side == 0 else cs

            @pl.loop(0, SUB)
            def _(i):
                c = first_col + lax.rem(cs + i, SUB)
                src = emsg.at[slot_rows(c), :]

                @pl.when(c != cs)
                def _():
                    remote(
                        src, ebuf.at[slot_rows(HALO + edge_at), :], e_send, e_recv,
                        plane * columns + c,
                    ).start()

                @pl.when(edge_at < HALO)
                def _():
                    remote(
                        src, ebuf.at[slot_rows(columns + HALO + edge_at), :], h_send, e_recv,
                        below * columns + c,
                    ).start()

                @pl.when(edge_at >= columns - HALO)
                def _():
                    remote(
                        src, ebuf.at[slot_rows(edge_at - (columns - HALO)), :], h_send, e_recv,
                        above * columns + c,
                    ).start()

        for side in range(2):
            gee_copy(side, k).start()

    shift = (cs < half).astype(jnp.int32)
    ebuf[slot_rows(here - shift), :] = emsg[slot_rows(cs), :]

    await_bytes(lbuf.at[pl.ds(0, rows_w - 1)], l_recv)
    await_bytes(ebuf.at[pl.ds(0, (rows_w - 1) * SUB), :], e_recv)
    for f in range(8):
        for t in range(rows_w // SUB):
            edge[f, SUB * (t + 1) : SUB * (t + 2), :] = ebuf[
                pl.ds(f + SUB * SUB * t, SUB, stride=SUB), :
            ]
    loc_w = [lbuf[:, f, :] for f in range(2)]
    for f in range(2):
        edge[8 + f, SUB : SUB + rows_w, :] = loc_w[f]

    def step(t, kappa):
        now = lax.rem(t, 2)
        size = jnp.zeros((SUB, LANES), F32)
        for w in range(rows_w // SUB):
            cut = slice(SUB * w, SUB * (w + 1))
            mid = slice(SUB * (w + 1), SUB * (w + 2))
            low = slice(SUB * (w + 1) - 1, SUB * (w + 2) - 1)
            high = slice(SUB * (w + 1) + 1, SUB * (w + 2) + 1)
            u = [vec[now, f, mid, :] for f in range(4)]
            u_low = [vec[now, f, low, :] for f in range(4)]
            u_high = [vec[now, f, high, :] for f in range(4)]
            lr, li = edge[8, mid, :], edge[9, mid, :]
            for a in range(2):
                d = deg[a, cut, :]
                o = 1 - a
                sign = 1.0 if a == 0 else -1.0
                re = d * u[2 * a] + lr * u[2 * o] - sign * (li * u[2 * o + 1])
                im = d * u[2 * a + 1] + lr * u[2 * o + 1] + sign * (li * u[2 * o])
                for b in range(2):
                    f = (2 * a + b) * 2
                    gr, gi = edge[f, mid, :], edge[f + 1, mid, :]
                    re = re + (gr * u_high[2 * b] - gi * u_high[2 * b + 1])
                    im = im + (gr * u_high[2 * b + 1] + gi * u_high[2 * b])
                    f = (2 * b + a) * 2
                    gr, gi = edge[f, low, :], edge[f + 1, low, :]
                    re = re + (gr * u_low[2 * b] + gi * u_low[2 * b + 1])
                    im = im + (gr * u_low[2 * b + 1] - gi * u_low[2 * b])
                vec[1 - now, 2 * a, mid, :] = re
                vec[1 - now, 2 * a + 1, mid, :] = im
                if HALO // SUB <= w < (HALO + columns) // SUB:
                    size = size + (re * re + im * im)
        return (jnp.sum(size, axis=0, keepdims=True) + EPS * kappa) / acq_total

    kappa = lax.fori_loop(0, ITERS, step, jnp.full((1, LANES), 1.0 / planes, F32))
    last = ITERS % 2
    nmsg[0:1, :] = kappa

    qual = jnp.zeros((SUB, LANES), F32)
    for w in range(HALO // SUB, (HALO + columns) // SUB):
        mid = slice(SUB * (w + 1), SUB * (w + 2))
        high = slice(SUB * (w + 1) + 1, SUB * (w + 2) + 1)
        u = [vec[last, f, mid, :] for f in range(4)]
        u_high = [vec[last, f, high, :] for f in range(4)]
        qual = qual + edge[8, mid, :] * (u[0] * u[2] + u[1] * u[3])
        qual = qual - edge[9, mid, :] * (u[0] * u[3] - u[1] * u[2])
        for a in range(2):
            for b in range(2):
                f = (2 * a + b) * 2
                ur, ui = u[2 * a], u[2 * a + 1]
                vr, vi = u_high[2 * b], u_high[2 * b + 1]
                qual = qual + edge[f, mid, :] * (ur * vr + ui * vi)
                qual = qual - edge[f + 1, mid, :] * (ur * vi - ui * vr)
    nmsg[1:2, :] = jnp.sum(qual, axis=0, keepdims=True)
    for i in range(1, planes):
        target = lax.rem(plane + i, planes) * columns + cs
        remote(nmsg, nbuf.at[plane], n_send, n_recv, target).start()
    own = slice(SUB + HALO, SUB + HALO + columns)
    for f in range(4):
        umsg[:, f, :] = vec[last, f, own, :]

    @pl.loop(1, columns)
    def _(i):
        c = lax.rem(cs + i, columns)
        remote(umsg.at[c], ubuf.at[cs], u_send, u_recv, plane * columns + c).start()

    nbuf[plane] = nmsg[...]
    ubuf[cs] = umsg[cs]

    for side in range(2):
        for k in range(2):
            gee_copy(side, k).wait_recv()
    for slot in range(4):
        hit_own = slot_key[slot] == code_own
        hits = [[slot_key[slot] == c for c in side] for side in codes]

        @pl.loop(0, columns // SUB)
        def _(g):
            cut = pl.ds(pl.multiple_of(g * SUB, SUB), SUB)
            for part in range(2):
                value = jnp.where(hit_own, loc[part, cut, :], 0.0)
                for side in range(2):
                    for c in range(4):
                        value = jnp.where(hits[side][c], gee[side, 2 * c + part, cut, :], value)
                ifg_ref[slot, part, cut, :] = value

    await_bytes(nbuf.at[pl.ds(0, planes - 1)], n_recv)
    both = nbuf[0]
    for i in range(1, planes):
        both = both + nbuf[i]
    kappa, qual = both[0:1, :], both[1:2, :]
    amsg[0:1, :] = 1.0 / jnp.sqrt(kappa)
    amsg[1:2, :] = qual / (kappa * pairs_total)

    @pl.loop(1, columns)
    def _(i):
        c = lax.rem(cs + i, columns)
        remote(amsg, abuf.at[cs], a_send, a_recv, plane * columns + c).start()

    abuf[cs] = amsg[...]

    tile = lax.broadcasted_iota(jnp.int32, (1, LANES), 1).astype(F32)
    free = jnp.where(tile_tab[...] == me, tile, big)
    picks = []
    for _ in range(TILE_CAP):
        first = jnp.min(free, axis=1, keepdims=True)
        hit = tile == first
        picks.append(jnp.where(hit, 1.0, 0.0))
        free = jnp.where(hit, big, free)

    await_bytes(ubuf.at[pl.ds(0, columns - 1)], u_recv)
    await_bytes(abuf.at[pl.ds(0, columns - 1)], a_recv)
    alpha = abuf[:, 0, :]
    for a in range(2):
        for part in range(2):
            link_ref[a, part] = ubuf[:, 2 * a + part, :] * alpha
    quality = abuf[:, 1, :]
    pick = jnp.concatenate(picks + [jnp.zeros((SUB - TILE_CAP, LANES), F32)], axis=0)
    chosen = lax.dot_general(
        pick, quality, (((1,), (1,)), ((), ())),
        precision=lax.Precision.HIGHEST, preferred_element_type=F32,
    )
    for a in range(TILE_CAP):
        qual_ref[a] = chosen[a : a + 1, :]

    for side in range(2):
        for k in range(2):
            sample_copy(side, k).wait_send()
            gee_copy(side, k).wait_send()
    await_bytes(lmsg.at[pl.ds(0, columns - 1)], l_send)
    await_bytes(emsg.at[pl.ds(0, (columns - 1) * SUB), :], e_send)
    await_bytes(ubuf.at[pl.ds(0, columns - 1)], u_send)
    await_bytes(abuf.at[pl.ds(0, columns - 1)], a_send)
    await_bytes(nbuf.at[pl.ds(0, planes - 1)], n_send)

    @pl.when(jnp.logical_or(cs < HALO, cs >= columns - HALO))
    def _():
        await_bytes(lmsg, lh_send)

    for side in range(2):
        edge_at = cs - 1 if side == 0 else cs

        @pl.when(jnp.logical_or(edge_at < HALO, edge_at >= columns - HALO))
        def _():
            await_bytes(emsg.at[pl.ds(0, half * SUB), :], h_send)


def write_out(ifg_in, link_in, qual_in, ifg_out, link_out, qual_out, sem):
    copies = [
        pltpu.make_async_copy(src, dst, sem.at[i])
        for i, (src, dst) in enumerate(
            ((ifg_in, ifg_out), (link_in, link_out), (qual_in, qual_out))
        )
    ]
    for copy in copies:
        copy.start()
    for copy in copies:
        copy.wait()


def per_device(slc_amplitude, slc_phase, pair_list, pair_owner, tile_map):
    columns = slc_amplitude.shape[1] // LOOK
    raw = slc_amplitude.shape[2]
    pairs = pair_list.reshape(-1, LANES, 2).transpose(0, 2, 1)
    owners = pair_owner.reshape(-1, LANES)
    tiles = tile_map.reshape(-1, LANES)
    hbm = pl.BlockSpec(memory_space=pltpu.HBM)
    rows_w = columns + 2 * HALO
    dma = pltpu.SemaphoreType.DMA
    vmem = pl.BlockSpec(memory_space=pltpu.VMEM)
    arguments = (slc_amplitude, slc_phase, pairs, owners, tiles)
    results = pl.pallas_call(
        kernel,
        name="phase_linking",
        out_shape=(
            jax.ShapeDtypeStruct((4, 2, columns, LANES), F32),
            jax.ShapeDtypeStruct((2, 2, columns, LANES), F32),
            jax.ShapeDtypeStruct((TILE_CAP, 1, columns), F32),
        ),
        in_specs=[hbm] * 5,
        out_specs=(vmem, vmem, vmem),
        scratch_shapes=[
            pltpu.VMEM(slc_amplitude.shape, F32),
            pltpu.VMEM(slc_amplitude.shape, F32),
            pltpu.VMEM(pairs.shape, jnp.int32),
            pltpu.VMEM(owners.shape, jnp.int32),
            pltpu.VMEM(tiles.shape, jnp.int32),
            pltpu.VMEM((4, 4, raw // LANES, GROUP, LANES), F32),
            pltpu.VMEM((2, 4, raw // LANES, GROUP, LANES), F32),
            pltpu.VMEM((2, 4, raw // LANES, GROUP, LANES), F32),
            pltpu.VMEM((10 * SUB, raw), F32),
            pltpu.VMEM((raw, LANES), BF16),
            pltpu.VMEM((2, 8, columns, LANES), F32),
            pltpu.VMEM((2, columns, LANES), F32),
            pltpu.VMEM((2, columns, LANES), F32),
            pltpu.VMEM((columns * SUB, LANES), F32),
            pltpu.VMEM((rows_w * SUB, LANES), F32),
            pltpu.VMEM((columns, 2, LANES), F32),
            pltpu.VMEM((rows_w, 2, LANES), F32),
            pltpu.VMEM((10, rows_w + 2 * SUB, LANES), F32),
            pltpu.VMEM((2, 4, rows_w + 2 * SUB, LANES), F32),
            pltpu.VMEM((2, rows_w, LANES), F32),
            pltpu.VMEM((columns, 4, LANES), F32),
            pltpu.VMEM((columns, 4, LANES), F32),
            pltpu.VMEM((2, LANES), F32),
            pltpu.VMEM((4, 2, LANES), F32),
            pltpu.VMEM((2, LANES), F32),
            pltpu.VMEM((columns, 2, LANES), F32),
            dma((2, 4)), dma((3,)), dma((2, 2)), dma((2, 2)), dma((2, 2)), dma((2, 2)),
            dma, dma, dma, dma, dma, dma, dma, dma, dma, dma, dma, dma,
        ],
        compiler_params=pltpu.CompilerParams(
            collective_id=0, has_side_effects=True, vmem_limit_bytes=40 * 2**20
        ),
    )(*[pltpu.with_memory_space_constraint(x, pltpu.HBM) for x in arguments])
    return pl.pallas_call(
        write_out,
        name="write_out",
        out_shape=[jax.ShapeDtypeStruct(x.shape, F32) for x in results],
        in_specs=[vmem] * 3,
        out_specs=[hbm] * 3,
        scratch_shapes=[dma((3,))],
        compiler_params=pltpu.CompilerParams(vmem_limit_bytes=2**20),
    )(*results)


def solution(mesh):
    in_specs = (P("acq", None, "slab"), P("acq", None, "slab"), P(), P(), P())
    out_specs = (P("acq", None, None, "slab"), P("acq", None, None, "slab"), P("acq", "slab", None))
    return jax.shard_map(
        per_device, mesh=mesh, in_specs=in_specs, out_specs=out_specs, check_vma=False
    )
```

```python
from functools import partial

import jax
import jax.numpy as jnp
from jax import lax
from jax.experimental import pallas as pl
from jax.experimental.pallas import tpu as pltpu
from jax.sharding import PartitionSpec as P

MESH = pl.DeviceIdType.MESH
F32 = jnp.float32
BF16 = jnp.bfloat16
LOOK = 5
ITERS = 8
TILE_CAP = 2
EPS = 1e-06
BACK = 6
SLOT = 16
ROWS = 10
HALO = 8
LANES = 128
SUB = 8
GROUP = SUB * LOOK


def sincos(x):
    turns = jnp.floor(x * 0.6366197723675814 + 0.5)
    r = ((x - turns * 1.5703125) - turns * 4.837512969970703e-4) - turns * 7.54978995489188e-8
    z = r * r
    s = ((-1.9515295891e-4 * z + 8.3321608736e-3) * z - 1.6666654611e-1) * z * r + r
    c = ((2.443315711809948e-5 * z - 1.388731625493765e-3) * z + 4.166664568298827e-2) * z * z
    c = c - 0.5 * z + 1.0
    quarter = turns.astype(jnp.int32)
    odd = (quarter & 1) == 1
    sin = jnp.where(odd, c, s)
    cos = jnp.where(odd, s, c)
    sin = jnp.where((quarter & 2) == 2, -sin, sin)
    cos = jnp.where(((quarter + 1) & 2) == 2, -cos, cos)
    return sin, cos


def total(x):
    return jnp.sum(jnp.sum(x, axis=1, keepdims=True), axis=0, keepdims=True)


def smallest(x):
    return jnp.min(jnp.min(x, axis=1, keepdims=True), axis=0, keepdims=True)


def kernel(
    amp_hbm, ph_hbm, pair_hbm, owner_hbm, tile_hbm, ifg_ref, link_ref, qual_ref,
    amp, ph, pair_tab, owner_tab, tile_tab, smp, from_left, from_right, acc, win, gee, power, loc, emsg, ebuf,
    edge, vec, deg, umsg, ubuf, nmsg, nbuf, pick, chosen,
    in_sem, tab_sem, s_send, s_recv, g_send, g_recv, ready,
    e_send, h_send, e_recv, u_send, u_recv, n_send, n_recv,
):
    devices = lax.axis_size("acq")
    columns = loc.shape[1]
    planes = devices // columns
    half = columns // 2
    rows_w = columns + 2 * HALO
    lane_tiles = smp.shape[2]
    pairs_total = 4 * devices
    acq_total = 2 * devices
    me = lax.axis_index("acq")
    plane = me // columns
    cs = lax.rem(me, columns)
    right = lax.rem(me + 1, devices)
    left = lax.rem(me + devices - 1, devices)
    above = lax.rem(plane + 1, planes)
    below = lax.rem(plane + planes - 1, planes)

    def remote(src, dst, send, recv, target):
        return pltpu.make_async_remote_copy(
            src_ref=src, dst_ref=dst, send_sem=send, recv_sem=recv,
            device_id={"acq": target}, device_id_type=MESH,
        )

    def await_bytes(ref, sem):
        pltpu.make_async_copy(ref, ref, sem).wait()

    order = (0, 2, 1, 3)
    for g in order:
        for a, (src, dst) in enumerate(((amp_hbm, amp), (ph_hbm, ph))):
            cut = pl.ds(g * GROUP, GROUP)
            pltpu.make_async_copy(src.at[:, cut, :], dst.at[:, cut, :], in_sem.at[a, g]).start()

    tables = ((pair_hbm, pair_tab), (owner_hbm, owner_tab), (tile_hbm, tile_tab))
    for i, (src, dst) in enumerate(tables):
        pltpu.make_async_copy(src, dst, tab_sem.at[i]).start()

    barrier = pltpu.get_barrier_semaphore()

    def tell(target):
        pl.semaphore_signal(barrier, inc=1, device_id={"acq": target}, device_id_type=MESH)

    tell(left)
    tell(right)

    def say(r):
        for target in (me + 2**r, me + devices - 2**r):
            pl.semaphore_signal(
                ready.at[r], inc=1, device_id={"acq": lax.rem(target, devices)},
                device_id_type=MESH,
            )

    def hear(r):
        pl.semaphore_wait(ready.at[r], 2)

    def form_samples(g):
        for a, (src, dst) in enumerate(((amp_hbm, amp), (ph_hbm, ph))):
            cut = pl.ds(g * GROUP, GROUP)
            pltpu.make_async_copy(src.at[:, cut, :], dst.at[:, cut, :], in_sem.at[a, g]).wait()

        @pl.loop(0, LOOK)
        def _(i):
            cut = pl.ds(pl.multiple_of(g * GROUP + i * SUB, SUB), SUB)
            here = pl.ds(pl.multiple_of(i * SUB, SUB), SUB)
            for a in range(2):
                size = amp[a, cut, :]
                sin, cos = sincos(ph[a, cut, :])
                real, imag = size * cos, size * sin
                for lt in range(lane_tiles):
                    lanes = slice(lt * LANES, (lt + 1) * LANES)
                    smp[g, 2 * a, lt, here, :] = real[:, lanes]
                    smp[g, 2 * a + 1, lt, here, :] = imag[:, lanes]

    def sample_copy(side, k):
        if side == 0:
            return remote(smp.at[k], from_left.at[k], s_send.at[0, k], s_recv.at[0, k], right)
        return remote(smp.at[2 + k], from_right.at[k], s_send.at[1, k], s_recv.at[1, k], left)

    form_samples(0)
    form_samples(2)
    pl.semaphore_wait(barrier, 2)
    sample_copy(0, 0).start()
    sample_copy(1, 0).start()
    say(0)
    form_samples(1)
    form_samples(3)
    sample_copy(0, 1).start()
    sample_copy(1, 1).start()

    hear(0)
    say(1)

    raw = lax.broadcasted_iota(jnp.int32, win.shape, 0)
    low = lax.broadcasted_iota(jnp.int32, win.shape, 1) * LOOK
    win[...] = jnp.where((raw >= low) & (raw < low + LOOK), 1.0, 0.0).astype(BF16)

    def look(count):
        x = acc[0:count, :]
        high = x.astype(BF16)
        rest = (x - high.astype(F32)).astype(BF16)
        return jnp.dot(high, win[...], preferred_element_type=F32) + jnp.dot(
            rest, win[...], preferred_element_type=F32
        )

    hear(1)
    say(2)

    for i, (src, dst) in enumerate(tables):
        pltpu.make_async_copy(src, dst, tab_sem.at[i]).wait()
    pair_ref, pair_sec = pair_tab[:, 0, :], pair_tab[:, 1, :]
    key = pair_ref * 256 + pair_sec
    base = 2 * me

    def key_of(i, j):
        return (base + i) * 256 + base + j

    codes = [[key_of(i - 2, j) for i in range(2) for j in range(2)],
             [key_of(i, j + 2) for i in range(2) for j in range(2)]]
    code_own = key_of(0, 1)

    def count_of(code):
        return total(jnp.where(key == code, 1.0, 0.0))

    weight = [[count_of(c) for c in side] for side in codes]
    weight_own = count_of(code_own)

    index = (
        lax.broadcasted_iota(jnp.int32, (4, LANES), 0) * LANES
        + lax.broadcasted_iota(jnp.int32, (4, LANES), 1)
    ).astype(F32)
    key_f = key.astype(F32)
    big = 1e6
    left_over = jnp.where(owner_tab[...] == me, index, big)
    slot_key = []
    for _ in range(4):
        first = smallest(left_over)
        hit = index == first
        slot_key.append(total(jnp.where(hit, key_f, 0.0)).astype(jnp.int32))
        left_over = jnp.where(hit, big, left_over)

    hear(2)
    say(3)

    ones = jnp.ones((LANES, LANES), BF16)
    window_dev = lax.rem(
        lax.broadcasted_iota(jnp.int32, (rows_w, LANES), 0)
        + (plane * columns + devices - HALO),
        devices,
    )
    for i in range(2):
        acq = 2 * window_dev + i
        hits = jnp.zeros((rows_w, LANES), F32)
        for member in (pair_ref, pair_sec):
            for q in range(4):
                hits = hits + jnp.where(acq == member[q : q + 1, :], 1.0, 0.0)
        deg[i] = 1.0 + jnp.dot(hits.astype(BF16), ones, preferred_element_type=F32)

    tile = lax.broadcasted_iota(jnp.int32, (SUB, LANES), 1).astype(F32)
    place = lax.broadcasted_iota(jnp.int32, (SUB, LANES), 0)
    holder = (place // TILE_CAP) * columns + cs
    free = jnp.where(tile_tab[...] == holder, tile, big)
    first = jnp.min(free, axis=1, keepdims=True)
    second = jnp.min(jnp.where(tile == first, big, free), axis=1, keepdims=True)
    wanted = jnp.where(lax.rem(place, TILE_CAP) == 0, first, second)
    pick[...] = jnp.where(tile == wanted, 1.0, 0.0)

    hear(3)
    say(4)

    @pl.loop(0, 4)
    def _(g):
        @pl.loop(0, lane_tiles)
        def _(lt):
            lanes = pl.ds(pl.multiple_of(lt * LANES, LANES), LANES)
            sums = [jnp.zeros((SUB, LANES), F32) for _ in range(4)]
            for kk in range(LOOK):
                x = [smp[g, f, lt, pl.ds(kk, SUB, stride=LOOK), :] for f in range(4)]
                sums[0] = sums[0] + (x[0] * x[0] + x[1] * x[1])
                sums[1] = sums[1] + (x[2] * x[2] + x[3] * x[3])
                sums[2] = sums[2] + (x[0] * x[2] + x[1] * x[3])
                sums[3] = sums[3] + (x[1] * x[2] - x[0] * x[3])
            for f in range(4):
                acc[f * SUB : (f + 1) * SUB, lanes] = sums[f]

        out = look(4 * SUB)
        cut = pl.ds(pl.multiple_of(g * SUB, SUB), SUB)
        power_ref, power_sec = out[0:SUB], out[SUB : 2 * SUB]
        power[0, cut, :] = power_ref
        power[1, cut, :] = power_sec
        scale = 1.0 / jnp.sqrt(power_ref * power_sec)
        loc[0, cut, :] = out[2 * SUB : 3 * SUB] * scale
        loc[1, cut, :] = out[3 * SUB : 4 * SUB] * scale

    for f in range(2):
        for g in range(columns // SUB):
            emsg[pl.ds(SLOT * SUB * g + 8 + f, SUB, stride=SLOT), :] = (
                loc[f, SUB * g : SUB * (g + 1), :] * weight_own
            )

    hear(4)
    say(5)

    vec[...] = jnp.zeros_like(vec)
    vec[0, 0] = jnp.ones(vec.shape[2:], F32)
    vec[0, 2] = jnp.ones(vec.shape[2:], F32)
    for f in range(8):
        edge[f, 0:SUB, :] = jnp.zeros((SUB, LANES), F32)
    ebuf[0:SLOT, :] = jnp.zeros((SLOT, LANES), F32)

    def gee_copy(side, k):
        if side == 0:
            part = gee.at[0, :, pl.ds(SUB * k, SUB), :]
            return remote(
                part, gee.at[1, :, pl.ds(SUB * k, SUB), :], g_send.at[0, k], g_recv.at[0, k], left
            )
        part = gee.at[1, :, pl.ds(half + SUB * k, SUB), :]
        return remote(
            part, gee.at[0, :, pl.ds(half + SUB * k, SUB), :],
            g_send.at[1, k], g_recv.at[1, k], right,
        )

    def slot_rows(slot):
        return pl.ds(pl.multiple_of(SLOT * slot, SLOT), ROWS)

    def window_rows(slot):
        return slot_rows(slot + 1)

    hear(5)

    for k in range(2):
        for side in range(2):
            sample_copy(side, k).wait_recv()
            other = (from_left, from_right)[side]
            first_col = side * half + k * SUB

            @pl.loop(0, lane_tiles)
            def _(lt):
                lanes = pl.ds(pl.multiple_of(lt * LANES, LANES), LANES)
                sums = [jnp.zeros((SUB, LANES), F32) for _ in range(10)]
                for kk in range(LOOK):
                    cut = pl.ds(kk, SUB, stride=LOOK)
                    near = [smp[2 * side + k, f, lt, cut, :] for f in range(4)]
                    far = [other[k, f, lt, cut, :] for f in range(4)]
                    ref, sec = (far, near) if side == 0 else (near, far)
                    for i in range(2):
                        for j in range(2):
                            f = (2 * i + j) * 2
                            sums[f] = sums[f] + (
                                ref[2 * i] * sec[2 * j] + ref[2 * i + 1] * sec[2 * j + 1]
                            )
                            sums[f + 1] = sums[f + 1] + (
                                ref[2 * i + 1] * sec[2 * j] - ref[2 * i] * sec[2 * j + 1]
                            )
                        sums[8 + i] = sums[8 + i] + (
                            far[2 * i] * far[2 * i] + far[2 * i + 1] * far[2 * i + 1]
                        )
                for f in range(10):
                    acc[f * SUB : (f + 1) * SUB, lanes] = sums[f]

            out = look(10 * SUB)
            for i in range(2):
                for j in range(2):
                    mine, theirs = (j, i) if side == 0 else (i, j)
                    scale = 1.0 / jnp.sqrt(
                        power[mine, first_col : first_col + SUB, :]
                        * out[(8 + theirs) * SUB : (9 + theirs) * SUB]
                    )
                    for part in range(2):
                        f = (2 * i + j) * 2 + part
                        value = out[f * SUB : (f + 1) * SUB] * scale
                        gee[side, f, first_col : first_col + SUB, :] = value
                        emsg[pl.ds(SLOT * first_col + f, SUB, stride=SLOT), :] = (
                            value * weight[side][2 * i + j]
                        )

            edge_at = cs - 1 if side == 0 else cs

            @pl.loop(0, SUB)
            def _(i):
                c = first_col + lax.rem(cs + i, SUB)
                src = emsg.at[slot_rows(c), :]

                @pl.when(c != cs)
                def _():
                    remote(
                        src, ebuf.at[window_rows(HALO + edge_at), :], e_send, e_recv,
                        plane * columns + c,
                    ).start()

                @pl.when(edge_at < HALO)
                def _():
                    remote(
                        src, ebuf.at[window_rows(columns + HALO + edge_at), :], h_send, e_recv,
                        below * columns + c,
                    ).start()

                @pl.when(edge_at >= columns - HALO)
                def _():
                    remote(
                        src, ebuf.at[window_rows(edge_at - (columns - HALO)), :], h_send, e_recv,
                        above * columns + c,
                    ).start()

        for side in range(2):
            gee_copy(side, k).start()

    shift = (cs < half).astype(jnp.int32)
    ebuf[window_rows(HALO + cs - shift), :] = emsg[slot_rows(cs), :]

    await_bytes(ebuf.at[pl.ds(0, (rows_w - 1) * ROWS), :], e_recv)
    for f in range(ROWS):
        back_by = shift if f >= 8 else 0
        for t in range(rows_w // SUB):
            edge[f, SUB * (t + 1) : SUB * (t + 2), :] = ebuf[
                pl.ds(f + SLOT * (SUB * t + 1 - back_by), SUB, stride=SLOT), :
            ]

    def step(t, kappa):
        now = lax.rem(t, 2)
        size = jnp.zeros((SUB, LANES), F32)
        for w in range(rows_w // SUB):
            cut = slice(SUB * w, SUB * (w + 1))
            mid = slice(SUB * (w + 1), SUB * (w + 2))
            low = slice(SUB * (w + 1) - 1, SUB * (w + 2) - 1)
            high = slice(SUB * (w + 1) + 1, SUB * (w + 2) + 1)
            u = [vec[now, f, mid, :] for f in range(4)]
            u_low = [vec[now, f, low, :] for f in range(4)]
            u_high = [vec[now, f, high, :] for f in range(4)]
            lr, li = edge[8, mid, :], edge[9, mid, :]
            for a in range(2):
                d = deg[a, cut, :]
                o = 1 - a
                sign = 1.0 if a == 0 else -1.0
                re = d * u[2 * a] + lr * u[2 * o] - sign * (li * u[2 * o + 1])
                im = d * u[2 * a + 1] + lr * u[2 * o + 1] + sign * (li * u[2 * o])
                for b in range(2):
                    f = (2 * a + b) * 2
                    gr, gi = edge[f, mid, :], edge[f + 1, mid, :]
                    re = re + (gr * u_high[2 * b] - gi * u_high[2 * b + 1])
                    im = im + (gr * u_high[2 * b + 1] + gi * u_high[2 * b])
                    f = (2 * b + a) * 2
                    gr, gi = edge[f, low, :], edge[f + 1, low, :]
                    re = re + (gr * u_low[2 * b] + gi * u_low[2 * b + 1])
                    im = im + (gr * u_low[2 * b + 1] - gi * u_low[2 * b])
                vec[1 - now, 2 * a, mid, :] = re
                vec[1 - now, 2 * a + 1, mid, :] = im
                if HALO // SUB <= w < (HALO + columns) // SUB:
                    size = size + (re * re + im * im)
        return (jnp.sum(size, axis=0, keepdims=True) + EPS * kappa) / acq_total

    kappa = lax.fori_loop(0, ITERS, step, jnp.full((1, LANES), 1.0 / planes, F32))
    last = ITERS % 2
    qual = jnp.zeros((SUB, LANES), F32)
    for w in range(HALO // SUB, (HALO + columns) // SUB):
        mid = slice(SUB * (w + 1), SUB * (w + 2))
        high = slice(SUB * (w + 1) + 1, SUB * (w + 2) + 1)
        u = [vec[last, f, mid, :] for f in range(4)]
        u_high = [vec[last, f, high, :] for f in range(4)]
        qual = qual + edge[8, mid, :] * (u[0] * u[2] + u[1] * u[3])
        qual = qual - edge[9, mid, :] * (u[0] * u[3] - u[1] * u[2])
        for a in range(2):
            for b in range(2):
                f = (2 * a + b) * 2
                ur, ui = u[2 * a], u[2 * a + 1]
                vr, vi = u_high[2 * b], u_high[2 * b + 1]
                qual = qual + edge[f, mid, :] * (ur * vr + ui * vi)
                qual = qual - edge[f + 1, mid, :] * (ur * vi - ui * vr)
    qual = jnp.sum(qual, axis=0, keepdims=True)

    for g in range(columns // SUB):
        cut = slice(SUB + HALO + SUB * g, SUB + HALO + SUB * (g + 1))
        for f in range(4):
            umsg[pl.ds(SUB * SUB * g + f, SUB, stride=SUB), :] = vec[last, f, cut, :]
        umsg[pl.ds(SUB * SUB * g + 4, SUB, stride=SUB), :] = jnp.broadcast_to(kappa, (SUB, LANES))
        umsg[pl.ds(SUB * SUB * g + 5, SUB, stride=SUB), :] = jnp.broadcast_to(qual, (SUB, LANES))

    def back_rows(slot):
        return pl.ds(pl.multiple_of(SUB * slot, SUB), BACK)

    @pl.loop(1, columns)
    def _(i):
        c = lax.rem(cs + i, columns)
        remote(
            umsg.at[back_rows(c), :], ubuf.at[back_rows(cs), :], u_send, u_recv,
            plane * columns + c,
        ).start()

    ubuf[back_rows(cs), :] = umsg[back_rows(cs), :]

    for side in range(2):
        for k in range(2):
            gee_copy(side, k).wait_recv()
    for slot in range(4):
        hit_own = slot_key[slot] == code_own
        hits = [[slot_key[slot] == c for c in side] for side in codes]

        @pl.loop(0, columns // SUB)
        def _(g):
            cut = pl.ds(pl.multiple_of(g * SUB, SUB), SUB)
            for part in range(2):
                value = jnp.where(hit_own, loc[part, cut, :], 0.0)
                for side in range(2):
                    for c in range(4):
                        value = jnp.where(hits[side][c], gee[side, 2 * c + part, cut, :], value)
                ifg_ref[slot, part, cut, :] = value

    def back(f, g):
        return ubuf[pl.ds(SUB * SUB * g + f, SUB, stride=SUB), :]

    def picked(x):
        return lax.dot_general(
            pick[...], x, (((1,), (1,)), ((), ())),
            precision=lax.Precision.HIGHEST, preferred_element_type=F32,
        )

    await_bytes(ubuf.at[pl.ds(0, (columns - 1) * BACK), :], u_recv)
    for g in range(columns // SUB):
        nmsg[SUB * g : SUB * (g + 1), :] = back(4, g)
    quality = jnp.concatenate([back(5, g) for g in range(columns // SUB)], axis=0)
    nmsg[columns : columns + SUB, 0:columns] = picked(quality)
    nmsg[columns : columns + SUB, columns:] = jnp.zeros((SUB, LANES - columns), F32)
    for i in range(1, planes):
        target = lax.rem(plane + i, planes) * columns + cs
        remote(nmsg, nbuf.at[plane], n_send, n_recv, target).start()
    nbuf[plane] = nmsg[...]

    await_bytes(nbuf.at[pl.ds(0, planes - 1)], n_recv)
    scale = nbuf[0]
    for i in range(1, planes):
        scale = scale + nbuf[i]
    kappa = scale[0:columns]
    alpha = 1.0 / jnp.sqrt(kappa)
    for g in range(columns // SUB):
        cut = slice(SUB * g, SUB * (g + 1))
        for f in range(4):
            link_ref[f // 2, f % 2, cut, :] = back(f, g) * alpha[cut]
    norm = picked(kappa) * pairs_total
    held = norm > 0.0
    chosen[...] = jnp.where(
        held, scale[columns:, 0:columns] / jnp.where(held, norm, 1.0), 0.0
    )
    for a in range(TILE_CAP):
        qual_ref[a] = chosen[pl.ds(plane * TILE_CAP + a, 1), :]

    for side in range(2):
        for k in range(2):
            sample_copy(side, k).wait_send()
            gee_copy(side, k).wait_send()
    await_bytes(emsg.at[pl.ds(0, (columns - 1) * ROWS), :], e_send)
    await_bytes(ubuf.at[pl.ds(0, (columns - 1) * BACK), :], u_send)
    await_bytes(nbuf.at[pl.ds(0, planes - 1)], n_send)

    for side in range(2):
        edge_at = cs - 1 if side == 0 else cs

        @pl.when(jnp.logical_or(edge_at < HALO, edge_at >= columns - HALO))
        def _():
            await_bytes(emsg.at[pl.ds(0, half * ROWS), :], h_send)


def write_out(ifg_in, link_in, qual_in, ifg_out, link_out, qual_out, sem):
    copies = [
        pltpu.make_async_copy(src, dst, sem.at[i])
        for i, (src, dst) in enumerate(
            ((ifg_in, ifg_out), (link_in, link_out), (qual_in, qual_out))
        )
    ]
    for copy in copies:
        copy.start()
    for copy in copies:
        copy.wait()


def per_device(slc_amplitude, slc_phase, pair_list, pair_owner, tile_map):
    columns = slc_amplitude.shape[1] // LOOK
    raw = slc_amplitude.shape[2]
    pairs = pair_list.reshape(-1, LANES, 2).transpose(0, 2, 1)
    owners = pair_owner.reshape(-1, LANES)
    tiles = tile_map.reshape(-1, LANES)
    hbm = pl.BlockSpec(memory_space=pltpu.HBM)
    rows_w = columns + 2 * HALO
    planes = lax.axis_size("acq") // columns
    dma = pltpu.SemaphoreType.DMA
    vmem = pl.BlockSpec(memory_space=pltpu.VMEM)
    arguments = (slc_amplitude, slc_phase, pairs, owners, tiles)
    results = pl.pallas_call(
        kernel,
        name="phase_linking",
        out_shape=(
            jax.ShapeDtypeStruct((4, 2, columns, LANES), F32),
            jax.ShapeDtypeStruct((2, 2, columns, LANES), F32),
            jax.ShapeDtypeStruct((TILE_CAP, 1, columns), F32),
        ),
        in_specs=[hbm] * 5,
        out_specs=(vmem, vmem, vmem),
        scratch_shapes=[
            pltpu.VMEM(slc_amplitude.shape, F32),
            pltpu.VMEM(slc_amplitude.shape, F32),
            pltpu.VMEM(pairs.shape, jnp.int32),
            pltpu.VMEM(owners.shape, jnp.int32),
            pltpu.VMEM(tiles.shape, jnp.int32),
            pltpu.VMEM((4, 4, raw // LANES, GROUP, LANES), F32),
            pltpu.VMEM((2, 4, raw // LANES, GROUP, LANES), F32),
            pltpu.VMEM((2, 4, raw // LANES, GROUP, LANES), F32),
            pltpu.VMEM((10 * SUB, raw), F32),
            pltpu.VMEM((raw, LANES), BF16),
            pltpu.VMEM((2, 8, columns, LANES), F32),
            pltpu.VMEM((2, columns, LANES), F32),
            pltpu.VMEM((2, columns, LANES), F32),
            pltpu.VMEM((columns * SLOT, LANES), F32),
            pltpu.VMEM(((rows_w + 1) * SLOT, LANES), F32),
            pltpu.VMEM((10, rows_w + 2 * SUB, LANES), F32),
            pltpu.VMEM((2, 4, rows_w + 2 * SUB, LANES), F32),
            pltpu.VMEM((2, rows_w, LANES), F32),
            pltpu.VMEM((columns * SUB, LANES), F32),
            pltpu.VMEM((columns * SUB, LANES), F32),
            pltpu.VMEM((columns + SUB, LANES), F32),
            pltpu.VMEM((planes, columns + SUB, LANES), F32),
            pltpu.VMEM((SUB, LANES), F32),
            pltpu.VMEM((SUB, columns), F32),
            dma((2, 4)), dma((3,)), dma((2, 2)), dma((2, 2)), dma((2, 2)), dma((2, 2)),
            pltpu.SemaphoreType.REGULAR((6,)), dma, dma, dma, dma, dma, dma, dma,
        ],
        compiler_params=pltpu.CompilerParams(
            collective_id=0, has_side_effects=True, vmem_limit_bytes=40 * 2**20
        ),
    )(*[pltpu.with_memory_space_constraint(x, pltpu.HBM) for x in arguments])
    return pl.pallas_call(
        write_out,
        name="write_out",
        out_shape=[jax.ShapeDtypeStruct(x.shape, F32) for x in results],
        in_specs=[vmem] * 3,
        out_specs=[hbm] * 3,
        scratch_shapes=[dma((3,))],
        compiler_params=pltpu.CompilerParams(vmem_limit_bytes=2**20),
    )(*results)


def solution(mesh):
    in_specs = (P("acq", None, "slab"), P("acq", None, "slab"), P(), P(), P())
    out_specs = (P("acq", None, None, "slab"), P("acq", None, None, "slab"), P("acq", "slab", None))
    return jax.shard_map(
        per_device, mesh=mesh, in_specs=in_specs, out_specs=out_specs, check_vma=False
    )
```

```python
from functools import partial

import jax
import jax.numpy as jnp
from jax import lax
from jax.experimental import pallas as pl
from jax.experimental.pallas import tpu as pltpu
from jax.sharding import PartitionSpec as P

MESH = pl.DeviceIdType.MESH
F32 = jnp.float32
BF16 = jnp.bfloat16
LOOK = 5
ITERS = 8
TILE_CAP = 2
EPS = 1e-06
BACK = 6
SLOT = 16
ROWS = 10
HALO = 8
LANES = 128
SUB = 8
GROUP = SUB * LOOK


def sincos(x):
    turns = jnp.floor(x * 0.6366197723675814 + 0.5)
    r = ((x - turns * 1.5703125) - turns * 4.837512969970703e-4) - turns * 7.54978995489188e-8
    z = r * r
    s = ((-1.9515295891e-4 * z + 8.3321608736e-3) * z - 1.6666654611e-1) * z * r + r
    c = ((2.443315711809948e-5 * z - 1.388731625493765e-3) * z + 4.166664568298827e-2) * z * z
    c = c - 0.5 * z + 1.0
    quarter = turns.astype(jnp.int32)
    odd = (quarter & 1) == 1
    sin = jnp.where(odd, c, s)
    cos = jnp.where(odd, s, c)
    sin = jnp.where((quarter & 2) == 2, -sin, sin)
    cos = jnp.where(((quarter + 1) & 2) == 2, -cos, cos)
    return sin, cos


def total(x):
    return jnp.sum(jnp.sum(x, axis=1, keepdims=True), axis=0, keepdims=True)


def smallest(x):
    return jnp.min(jnp.min(x, axis=1, keepdims=True), axis=0, keepdims=True)


def kernel(
    amp_hbm, ph_hbm, pair_hbm, owner_hbm, tile_hbm, ifg_ref, link_ref, qual_ref,
    amp, ph, pair_tab, owner_tab, tile_tab, smp, from_left, from_right, acc, win, gee, power, loc, emsg, ebuf,
    edge, vec, deg, umsg, ubuf, nmsg, nbuf, pick, chosen,
    in_sem, tab_sem, s_send, s_recv, g_send, g_recv, ready,
    e_send, h_send, e_recv, u_send, u_recv, n_send, n_recv,
):
    devices = lax.axis_size("acq")
    columns = loc.shape[1]
    planes = devices // columns
    half = columns // 2
    rows_w = columns + 2 * HALO
    lane_tiles = smp.shape[2]
    pairs_total = 4 * devices
    acq_total = 2 * devices
    me = lax.axis_index("acq")
    assert columns & (columns - 1) == 0 and planes & (planes - 1) == 0

    def wrap(x, size):
        return x & (size - 1)

    plane = me >> (columns.bit_length() - 1)
    cs = wrap(me, columns)
    first_of_plane = me - cs
    right = wrap(me + 1, devices)
    left = wrap(me + devices - 1, devices)
    above = wrap(first_of_plane + columns, devices)
    below = wrap(first_of_plane + devices - columns, devices)

    def remote(src, dst, send, recv, target):
        return pltpu.make_async_remote_copy(
            src_ref=src, dst_ref=dst, send_sem=send, recv_sem=recv,
            device_id={"acq": target}, device_id_type=MESH,
        )

    def await_bytes(ref, sem):
        pltpu.make_async_copy(ref, ref, sem).wait()

    order = (0, 2, 1, 3)
    for g in order:
        for a, (src, dst) in enumerate(((amp_hbm, amp), (ph_hbm, ph))):
            cut = pl.ds(g * GROUP, GROUP)
            pltpu.make_async_copy(src.at[:, cut, :], dst.at[:, cut, :], in_sem.at[a, g]).start()

    tables = ((pair_hbm, pair_tab), (owner_hbm, owner_tab), (tile_hbm, tile_tab))
    for i, (src, dst) in enumerate(tables):
        pltpu.make_async_copy(src, dst, tab_sem.at[i]).start()

    barrier = pltpu.get_barrier_semaphore()

    def tell(target):
        pl.semaphore_signal(barrier, inc=1, device_id={"acq": target}, device_id_type=MESH)

    tell(left)
    tell(right)

    def say(r):
        for target in (me + 2**r, me + devices - 2**r):
            pl.semaphore_signal(
                ready.at[r], inc=1, device_id={"acq": wrap(target, devices)},
                device_id_type=MESH,
            )

    def hear(r):
        pl.semaphore_wait(ready.at[r], 2)

    def form_samples(g):
        for a, (src, dst) in enumerate(((amp_hbm, amp), (ph_hbm, ph))):
            cut = pl.ds(g * GROUP, GROUP)
            pltpu.make_async_copy(src.at[:, cut, :], dst.at[:, cut, :], in_sem.at[a, g]).wait()

        @pl.loop(0, LOOK)
        def _(i):
            cut = pl.ds(pl.multiple_of(g * GROUP + i * SUB, SUB), SUB)
            here = pl.ds(pl.multiple_of(i * SUB, SUB), SUB)
            for a in range(2):
                size = amp[a, cut, :]
                sin, cos = sincos(ph[a, cut, :])
                real, imag = size * cos, size * sin
                for lt in range(lane_tiles):
                    lanes = slice(lt * LANES, (lt + 1) * LANES)
                    smp[g, 2 * a, lt, here, :] = real[:, lanes]
                    smp[g, 2 * a + 1, lt, here, :] = imag[:, lanes]

    def sample_copy(side, k):
        if side == 0:
            return remote(smp.at[k], from_left.at[k], s_send.at[0, k], s_recv.at[0, k], right)
        return remote(smp.at[2 + k], from_right.at[k], s_send.at[1, k], s_recv.at[1, k], left)

    form_samples(0)
    form_samples(2)
    pl.semaphore_wait(barrier, 2)
    core = lax.axis_index("slab")
    say(0)

    @pl.when(core == 0)
    def _():
        sample_copy(0, 0).start()
        sample_copy(1, 0).start()

    form_samples(1)
    form_samples(3)

    @pl.when(core == 0)
    def _():
        sample_copy(0, 1).start()
        sample_copy(1, 1).start()

    @pl.when(core == 1)
    def _():
        sample_copy(0, 0).start()
        sample_copy(1, 0).start()

    hear(0)
    say(1)

    raw = lax.broadcasted_iota(jnp.int32, win.shape, 0)
    low = lax.broadcasted_iota(jnp.int32, win.shape, 1) * LOOK
    win[...] = jnp.where((raw >= low) & (raw < low + LOOK), 1.0, 0.0).astype(BF16)

    def look(count):
        x = acc[0:count, :]
        high = x.astype(BF16)
        rest = (x - high.astype(F32)).astype(BF16)
        return jnp.dot(high, win[...], preferred_element_type=F32) + jnp.dot(
            rest, win[...], preferred_element_type=F32
        )

    hear(1)
    say(2)

    for i, (src, dst) in enumerate(tables):
        pltpu.make_async_copy(src, dst, tab_sem.at[i]).wait()
    pair_ref, pair_sec = pair_tab[:, 0, :], pair_tab[:, 1, :]
    key = pair_ref * 256 + pair_sec
    base = 2 * me

    def key_of(i, j):
        return (base + i) * 256 + base + j

    codes = [[key_of(i - 2, j) for i in range(2) for j in range(2)],
             [key_of(i, j + 2) for i in range(2) for j in range(2)]]
    code_own = key_of(0, 1)

    def count_of(code):
        return total(jnp.where(key == code, 1.0, 0.0))

    weight = [[count_of(c) for c in side] for side in codes]
    weight_own = count_of(code_own)

    index = (
        lax.broadcasted_iota(jnp.int32, (4, LANES), 0) * LANES
        + lax.broadcasted_iota(jnp.int32, (4, LANES), 1)
    ).astype(F32)
    key_f = key.astype(F32)
    big = 1e6
    left_over = jnp.where(owner_tab[...] == me, index, big)
    slot_key = []
    for _ in range(4):
        first = smallest(left_over)
        hit = index == first
        slot_key.append(total(jnp.where(hit, key_f, 0.0)).astype(jnp.int32))
        left_over = jnp.where(hit, big, left_over)

    hear(2)
    say(3)

    ones = jnp.ones((LANES, LANES), BF16)
    window_dev = lax.rem(
        lax.broadcasted_iota(jnp.int32, (rows_w, LANES), 0)
        + (plane * columns + devices - HALO),
        devices,
    )
    for i in range(2):
        acq = 2 * window_dev + i
        hits = jnp.zeros((rows_w, LANES), F32)
        for member in (pair_ref, pair_sec):
            for q in range(4):
                hits = hits + jnp.where(acq == member[q : q + 1, :], 1.0, 0.0)
        deg[i] = 1.0 + jnp.dot(hits.astype(BF16), ones, preferred_element_type=F32)

    tile = lax.broadcasted_iota(jnp.int32, (SUB, LANES), 1).astype(F32)
    place = lax.broadcasted_iota(jnp.int32, (SUB, LANES), 0)
    holder = (place // TILE_CAP) * columns + cs
    free = jnp.where(tile_tab[...] == holder, tile, big)
    first = jnp.min(free, axis=1, keepdims=True)
    second = jnp.min(jnp.where(tile == first, big, free), axis=1, keepdims=True)
    wanted = jnp.where(lax.rem(place, TILE_CAP) == 0, first, second)
    pick[...] = jnp.where(tile == wanted, 1.0, 0.0)

    hear(3)
    say(4)

    @pl.when(core == 1)
    def _():
        sample_copy(0, 1).start()
        sample_copy(1, 1).start()

    @pl.loop(0, 4)
    def _(g):
        @pl.loop(0, lane_tiles)
        def _(lt):
            lanes = pl.ds(pl.multiple_of(lt * LANES, LANES), LANES)
            sums = [jnp.zeros((SUB, LANES), F32) for _ in range(4)]
            for kk in range(LOOK):
                x = [smp[g, f, lt, pl.ds(kk, SUB, stride=LOOK), :] for f in range(4)]
                sums[0] = sums[0] + (x[0] * x[0] + x[1] * x[1])
                sums[1] = sums[1] + (x[2] * x[2] + x[3] * x[3])
                sums[2] = sums[2] + (x[0] * x[2] + x[1] * x[3])
                sums[3] = sums[3] + (x[1] * x[2] - x[0] * x[3])
            for f in range(4):
                acc[f * SUB : (f + 1) * SUB, lanes] = sums[f]

        out = look(4 * SUB)
        cut = pl.ds(pl.multiple_of(g * SUB, SUB), SUB)
        power_ref, power_sec = out[0:SUB], out[SUB : 2 * SUB]
        power[0, cut, :] = power_ref
        power[1, cut, :] = power_sec
        scale = 1.0 / jnp.sqrt(power_ref * power_sec)
        loc[0, cut, :] = out[2 * SUB : 3 * SUB] * scale
        loc[1, cut, :] = out[3 * SUB : 4 * SUB] * scale

    for f in range(2):
        for g in range(columns // SUB):
            emsg[pl.ds(SLOT * SUB * g + 8 + f, SUB, stride=SLOT), :] = (
                loc[f, SUB * g : SUB * (g + 1), :] * weight_own
            )

    hear(4)
    say(5)

    vec[...] = jnp.zeros_like(vec)
    vec[0, 0] = jnp.ones(vec.shape[2:], F32)
    vec[0, 2] = jnp.ones(vec.shape[2:], F32)
    for f in range(8):
        edge[f, 0:SUB, :] = jnp.zeros((SUB, LANES), F32)
    ebuf[0:SLOT, :] = jnp.zeros((SLOT, LANES), F32)

    def gee_copy(side, k):
        if side == 0:
            part = gee.at[0, :, pl.ds(SUB * k, SUB), :]
            return remote(
                part, gee.at[1, :, pl.ds(SUB * k, SUB), :], g_send.at[0, k], g_recv.at[0, k], left
            )
        part = gee.at[1, :, pl.ds(half + SUB * k, SUB), :]
        return remote(
            part, gee.at[0, :, pl.ds(half + SUB * k, SUB), :],
            g_send.at[1, k], g_recv.at[1, k], right,
        )

    def slot_rows(slot):
        return pl.ds(pl.multiple_of(SLOT * slot, SLOT), ROWS)

    def window_rows(slot):
        return slot_rows(slot + 1)

    hear(5)


    for k in range(2):
        for side in range(2):
            sample_copy(side, k).wait_recv()
            other = (from_left, from_right)[side]
            first_col = side * half + k * SUB

            @pl.loop(0, lane_tiles)
            def _(lt):
                lanes = pl.ds(pl.multiple_of(lt * LANES, LANES), LANES)
                sums = [jnp.zeros((SUB, LANES), F32) for _ in range(10)]
                for kk in range(LOOK):
                    cut = pl.ds(kk, SUB, stride=LOOK)
                    near = [smp[2 * side + k, f, lt, cut, :] for f in range(4)]
                    far = [other[k, f, lt, cut, :] for f in range(4)]
                    ref, sec = (far, near) if side == 0 else (near, far)
                    for i in range(2):
                        for j in range(2):
                            f = (2 * i + j) * 2
                            sums[f] = sums[f] + (
                                ref[2 * i] * sec[2 * j] + ref[2 * i + 1] * sec[2 * j + 1]
                            )
                            sums[f + 1] = sums[f + 1] + (
                                ref[2 * i + 1] * sec[2 * j] - ref[2 * i] * sec[2 * j + 1]
                            )
                        sums[8 + i] = sums[8 + i] + (
                            far[2 * i] * far[2 * i] + far[2 * i + 1] * far[2 * i + 1]
                        )
                for f in range(10):
                    acc[f * SUB : (f + 1) * SUB, lanes] = sums[f]

            out = look(10 * SUB)
            for i in range(2):
                for j in range(2):
                    mine, theirs = (j, i) if side == 0 else (i, j)
                    scale = 1.0 / jnp.sqrt(
                        power[mine, first_col : first_col + SUB, :]
                        * out[(8 + theirs) * SUB : (9 + theirs) * SUB]
                    )
                    for part in range(2):
                        f = (2 * i + j) * 2 + part
                        value = out[f * SUB : (f + 1) * SUB] * scale
                        gee[side, f, first_col : first_col + SUB, :] = value
                        emsg[pl.ds(SLOT * first_col + f, SUB, stride=SLOT), :] = (
                            value * weight[side][2 * i + j]
                        )

            edge_at = cs - 1 if side == 0 else cs

            @pl.loop(0, SUB)
            def _(i):
                c = first_col + wrap(cs + i, SUB)
                src = emsg.at[slot_rows(c), :]

                @pl.when(edge_at < HALO)
                def _():
                    remote(
                        src, ebuf.at[window_rows(columns + HALO + edge_at), :], h_send, e_recv,
                        below + c,
                    ).start()

                @pl.when(edge_at >= columns - HALO)
                def _():
                    remote(
                        src, ebuf.at[window_rows(edge_at - (columns - HALO)), :], h_send, e_recv,
                        above + c,
                    ).start()

                @pl.when(c != cs)
                def _():
                    remote(
                        src, ebuf.at[window_rows(HALO + edge_at), :], e_send, e_recv,
                        first_of_plane + c,
                    ).start()

        for side in range(2):
            gee_copy(side, k).start()

    shift = (cs < half).astype(jnp.int32)
    ebuf[window_rows(HALO + cs - shift), :] = emsg[slot_rows(cs), :]

    await_bytes(ebuf.at[pl.ds(0, (rows_w - 1) * ROWS), :], e_recv)
    for f in range(ROWS):
        back_by = shift if f >= 8 else 0
        for t in range(rows_w // SUB):
            edge[f, SUB * (t + 1) : SUB * (t + 2), :] = ebuf[
                pl.ds(f + SLOT * (SUB * t + 1 - back_by), SUB, stride=SLOT), :
            ]

    def step(t, kappa):
        now = lax.rem(t, 2)
        size = jnp.zeros((SUB, LANES), F32)
        for w in range(rows_w // SUB):
            cut = slice(SUB * w, SUB * (w + 1))
            mid = slice(SUB * (w + 1), SUB * (w + 2))
            low = slice(SUB * (w + 1) - 1, SUB * (w + 2) - 1)
            high = slice(SUB * (w + 1) + 1, SUB * (w + 2) + 1)
            u = [vec[now, f, mid, :] for f in range(4)]
            u_low = [vec[now, f, low, :] for f in range(4)]
            u_high = [vec[now, f, high, :] for f in range(4)]
            lr, li = edge[8, mid, :], edge[9, mid, :]
            for a in range(2):
                d = deg[a, cut, :]
                o = 1 - a
                sign = 1.0 if a == 0 else -1.0
                re = d * u[2 * a] + lr * u[2 * o] - sign * (li * u[2 * o + 1])
                im = d * u[2 * a + 1] + lr * u[2 * o + 1] + sign * (li * u[2 * o])
                for b in range(2):
                    f = (2 * a + b) * 2
                    gr, gi = edge[f, mid, :], edge[f + 1, mid, :]
                    re = re + (gr * u_high[2 * b] - gi * u_high[2 * b + 1])
                    im = im + (gr * u_high[2 * b + 1] + gi * u_high[2 * b])
                    f = (2 * b + a) * 2
                    gr, gi = edge[f, low, :], edge[f + 1, low, :]
                    re = re + (gr * u_low[2 * b] + gi * u_low[2 * b + 1])
                    im = im + (gr * u_low[2 * b + 1] - gi * u_low[2 * b])
                vec[1 - now, 2 * a, mid, :] = re
                vec[1 - now, 2 * a + 1, mid, :] = im
                if HALO // SUB <= w < (HALO + columns) // SUB:
                    size = size + (re * re + im * im)
        return (jnp.sum(size, axis=0, keepdims=True) + EPS * kappa) / acq_total

    kappa = lax.fori_loop(0, ITERS, step, jnp.full((1, LANES), 1.0 / planes, F32))
    last = ITERS % 2
    qual = jnp.zeros((SUB, LANES), F32)
    for w in range(HALO // SUB, (HALO + columns) // SUB):
        mid = slice(SUB * (w + 1), SUB * (w + 2))
        high = slice(SUB * (w + 1) + 1, SUB * (w + 2) + 1)
        u = [vec[last, f, mid, :] for f in range(4)]
        u_high = [vec[last, f, high, :] for f in range(4)]
        qual = qual + edge[8, mid, :] * (u[0] * u[2] + u[1] * u[3])
        qual = qual - edge[9, mid, :] * (u[0] * u[3] - u[1] * u[2])
        for a in range(2):
            for b in range(2):
                f = (2 * a + b) * 2
                ur, ui = u[2 * a], u[2 * a + 1]
                vr, vi = u_high[2 * b], u_high[2 * b + 1]
                qual = qual + edge[f, mid, :] * (ur * vr + ui * vi)
                qual = qual - edge[f + 1, mid, :] * (ur * vi - ui * vr)
    qual = jnp.sum(qual, axis=0, keepdims=True)

    for g in range(columns // SUB):
        cut = slice(SUB + HALO + SUB * g, SUB + HALO + SUB * (g + 1))
        for f in range(4):
            umsg[pl.ds(SUB * SUB * g + f, SUB, stride=SUB), :] = vec[last, f, cut, :]
        umsg[pl.ds(SUB * SUB * g + 4, SUB, stride=SUB), :] = jnp.broadcast_to(kappa, (SUB, LANES))
        umsg[pl.ds(SUB * SUB * g + 5, SUB, stride=SUB), :] = jnp.broadcast_to(qual, (SUB, LANES))

    def back_rows(slot):
        return pl.ds(pl.multiple_of(SUB * slot, SUB), BACK)

    @pl.loop(1, columns)
    def _(i):
        c = wrap(cs + i, columns)
        remote(
            umsg.at[back_rows(c), :], ubuf.at[back_rows(cs), :], u_send, u_recv,
            first_of_plane + c,
        ).start()

    ubuf[back_rows(cs), :] = umsg[back_rows(cs), :]

    for side in range(2):
        for k in range(2):
            gee_copy(side, k).wait_recv()
    for slot in range(4):
        hit_own = slot_key[slot] == code_own
        hits = [[slot_key[slot] == c for c in side] for side in codes]

        @pl.loop(0, columns // SUB)
        def _(g):
            cut = pl.ds(pl.multiple_of(g * SUB, SUB), SUB)
            for part in range(2):
                value = jnp.where(hit_own, loc[part, cut, :], 0.0)
                for side in range(2):
                    for c in range(4):
                        value = jnp.where(hits[side][c], gee[side, 2 * c + part, cut, :], value)
                ifg_ref[slot, part, cut, :] = value

    def back(f, g):
        return ubuf[pl.ds(SUB * SUB * g + f, SUB, stride=SUB), :]

    def picked(x):
        return lax.dot_general(
            pick[...], x, (((1,), (1,)), ((), ())),
            precision=lax.Precision.HIGHEST, preferred_element_type=F32,
        )

    await_bytes(ubuf.at[pl.ds(0, (columns - 1) * BACK), :], u_recv)
    for g in range(columns // SUB):
        nmsg[SUB * g : SUB * (g + 1), :] = back(4, g)
    quality = jnp.concatenate([back(5, g) for g in range(columns // SUB)], axis=0)
    nmsg[columns : columns + SUB, 0:columns] = picked(quality)
    nmsg[columns : columns + SUB, columns:] = jnp.zeros((SUB, LANES - columns), F32)
    for i in range(1, planes):
        target = lax.rem(plane + i, planes) * columns + cs
        remote(nmsg, nbuf.at[plane], n_send, n_recv, target).start()
    nbuf[plane] = nmsg[...]

    await_bytes(nbuf.at[pl.ds(0, planes - 1)], n_recv)
    scale = nbuf[0]
    for i in range(1, planes):
        scale = scale + nbuf[i]
    kappa = scale[0:columns]
    alpha = 1.0 / jnp.sqrt(kappa)
    for g in range(columns // SUB):
        cut = slice(SUB * g, SUB * (g + 1))
        for f in range(4):
            link_ref[f // 2, f % 2, cut, :] = back(f, g) * alpha[cut]
    norm = picked(kappa) * pairs_total
    held = norm > 0.0
    chosen[...] = jnp.where(
        held, scale[columns:, 0:columns] / jnp.where(held, norm, 1.0), 0.0
    )
    for a in range(TILE_CAP):
        qual_ref[a] = chosen[pl.ds(plane * TILE_CAP + a, 1), :]

    for side in range(2):
        for k in range(2):
            sample_copy(side, k).wait_send()
            gee_copy(side, k).wait_send()
    await_bytes(emsg.at[pl.ds(0, (columns - 1) * ROWS), :], e_send)
    await_bytes(ubuf.at[pl.ds(0, (columns - 1) * BACK), :], u_send)
    await_bytes(nbuf.at[pl.ds(0, planes - 1)], n_send)

    for side in range(2):
        edge_at = cs - 1 if side == 0 else cs

        @pl.when(jnp.logical_or(edge_at < HALO, edge_at >= columns - HALO))
        def _():
            await_bytes(emsg.at[pl.ds(0, half * ROWS), :], h_send)


def write_out(ifg_in, link_in, qual_in, ifg_out, link_out, qual_out, sem):
    copies = [
        pltpu.make_async_copy(src, dst, sem.at[i])
        for i, (src, dst) in enumerate(
            ((ifg_in, ifg_out), (link_in, link_out), (qual_in, qual_out))
        )
    ]
    for copy in copies:
        copy.start()
    for copy in copies:
        copy.wait()


def per_device(slc_amplitude, slc_phase, pair_list, pair_owner, tile_map):
    columns = slc_amplitude.shape[1] // LOOK
    raw = slc_amplitude.shape[2]
    pairs = pair_list.reshape(-1, LANES, 2).transpose(0, 2, 1)
    owners = pair_owner.reshape(-1, LANES)
    tiles = tile_map.reshape(-1, LANES)
    hbm = pl.BlockSpec(memory_space=pltpu.HBM)
    rows_w = columns + 2 * HALO
    planes = lax.axis_size("acq") // columns
    dma = pltpu.SemaphoreType.DMA
    vmem = pl.BlockSpec(memory_space=pltpu.VMEM)
    arguments = (slc_amplitude, slc_phase, pairs, owners, tiles)
    results = pl.pallas_call(
        kernel,
        name="phase_linking",
        out_shape=(
            jax.ShapeDtypeStruct((4, 2, columns, LANES), F32),
            jax.ShapeDtypeStruct((2, 2, columns, LANES), F32),
            jax.ShapeDtypeStruct((TILE_CAP, 1, columns), F32),
        ),
        in_specs=[hbm] * 5,
        out_specs=(vmem, vmem, vmem),
        scratch_shapes=[
            pltpu.VMEM(slc_amplitude.shape, F32),
            pltpu.VMEM(slc_amplitude.shape, F32),
            pltpu.VMEM(pairs.shape, jnp.int32),
            pltpu.VMEM(owners.shape, jnp.int32),
            pltpu.VMEM(tiles.shape, jnp.int32),
            pltpu.VMEM((4, 4, raw // LANES, GROUP, LANES), F32),
            pltpu.VMEM((2, 4, raw // LANES, GROUP, LANES), F32),
            pltpu.VMEM((2, 4, raw // LANES, GROUP, LANES), F32),
            pltpu.VMEM((10 * SUB, raw), F32),
            pltpu.VMEM((raw, LANES), BF16),
            pltpu.VMEM((2, 8, columns, LANES), F32),
            pltpu.VMEM((2, columns, LANES), F32),
            pltpu.VMEM((2, columns, LANES), F32),
            pltpu.VMEM((columns * SLOT, LANES), F32),
            pltpu.VMEM(((rows_w + 1) * SLOT, LANES), F32),
            pltpu.VMEM((10, rows_w + 2 * SUB, LANES), F32),
            pltpu.VMEM((2, 4, rows_w + 2 * SUB, LANES), F32),
            pltpu.VMEM((2, rows_w, LANES), F32),
            pltpu.VMEM((columns * SUB, LANES), F32),
            pltpu.VMEM((columns * SUB, LANES), F32),
            pltpu.VMEM((columns + SUB, LANES), F32),
            pltpu.VMEM((planes, columns + SUB, LANES), F32),
            pltpu.VMEM((SUB, LANES), F32),
            pltpu.VMEM((SUB, columns), F32),
            dma((2, 4)), dma((3,)), dma((2, 2)), dma((2, 2)), dma((2, 2)), dma((2, 2)),
            pltpu.SemaphoreType.REGULAR((6,)), dma, dma, dma, dma, dma, dma, dma,
        ],
        compiler_params=pltpu.CompilerParams(
            collective_id=0, has_side_effects=True, vmem_limit_bytes=40 * 2**20
        ),
    )(*[pltpu.with_memory_space_constraint(x, pltpu.HBM) for x in arguments])
    return pl.pallas_call(
        write_out,
        name="write_out",
        out_shape=[jax.ShapeDtypeStruct(x.shape, F32) for x in results],
        in_specs=[vmem] * 3,
        out_specs=[hbm] * 3,
        scratch_shapes=[dma((3,))],
        compiler_params=pltpu.CompilerParams(vmem_limit_bytes=2**20),
    )(*results)


def solution(mesh):
    in_specs = (P("acq", None, "slab"), P("acq", None, "slab"), P(), P(), P())
    out_specs = (P("acq", None, None, "slab"), P("acq", None, None, "slab"), P("acq", "slab", None))
    return jax.shard_map(
        per_device, mesh=mesh, in_specs=in_specs, out_specs=out_specs, check_vma=False
    )
```

```python
from functools import partial

import jax
import jax.numpy as jnp
from jax import lax
from jax.experimental import pallas as pl
from jax.experimental.pallas import tpu as pltpu
from jax.sharding import PartitionSpec as P

MESH = pl.DeviceIdType.MESH
F32 = jnp.float32
BF16 = jnp.bfloat16
LOOK = 5
ITERS = 8
TILE_CAP = 2
EPS = 1e-06
BACK = 5
SLOT = 16
ROWS = 10
HALO = 8
LANES = 128
SUB = 8
GROUP = SUB * LOOK


def sincos(x):
    turns = jnp.floor(x * 0.6366197723675814 + 0.5)
    r = ((x - turns * 1.5703125) - turns * 4.837512969970703e-4) - turns * 7.54978995489188e-8
    z = r * r
    s = ((-1.9515295891e-4 * z + 8.3321608736e-3) * z - 1.6666654611e-1) * z * r + r
    c = ((2.443315711809948e-5 * z - 1.388731625493765e-3) * z + 4.166664568298827e-2) * z * z
    c = c - 0.5 * z + 1.0
    quarter = turns.astype(jnp.int32)
    odd = (quarter & 1) == 1
    sin = jnp.where(odd, c, s)
    cos = jnp.where(odd, s, c)
    sin = jnp.where((quarter & 2) == 2, -sin, sin)
    cos = jnp.where(((quarter + 1) & 2) == 2, -cos, cos)
    return sin, cos


def total(x):
    return jnp.sum(jnp.sum(x, axis=1, keepdims=True), axis=0, keepdims=True)


def smallest(x):
    return jnp.min(jnp.min(x, axis=1, keepdims=True), axis=0, keepdims=True)


def kernel(
    amp_hbm, ph_hbm, pair_hbm, owner_hbm, tile_hbm, ifg_ref, link_ref, qual_ref,
    amp, ph, pair_tab, owner_tab, tile_tab, smp, from_left, from_right, acc, win, gee, power, loc, emsg, ebuf,
    edge, vec, deg, umsg, ubuf, nmsg, nbuf, pick, chosen,
    in_sem, tab_sem, s_send, s_recv, g_send, g_recv, ready,
    e_send, h_send, e_recv, u_send, u_recv, n_send, n_recv,
):
    devices = lax.axis_size("acq")
    columns = loc.shape[1]
    planes = devices // columns
    half = columns // 2
    rows_w = columns + 2 * HALO
    lane_tiles = smp.shape[2]
    pairs_total = 4 * devices
    acq_total = 2 * devices
    me = lax.axis_index("acq")
    assert columns & (columns - 1) == 0 and planes & (planes - 1) == 0

    def wrap(x, size):
        return x & (size - 1)

    plane = me >> (columns.bit_length() - 1)
    cs = wrap(me, columns)
    first_of_plane = me - cs
    right = wrap(me + 1, devices)
    left = wrap(me + devices - 1, devices)
    above = wrap(first_of_plane + columns, devices)
    below = wrap(first_of_plane + devices - columns, devices)

    def remote(src, dst, send, recv, target):
        return pltpu.make_async_remote_copy(
            src_ref=src, dst_ref=dst, send_sem=send, recv_sem=recv,
            device_id={"acq": target}, device_id_type=MESH,
        )

    def await_bytes(ref, sem):
        pltpu.make_async_copy(ref, ref, sem).wait()

    order = (0, 2, 1, 3)
    for g in order:
        for a, (src, dst) in enumerate(((amp_hbm, amp), (ph_hbm, ph))):
            cut = pl.ds(g * GROUP, GROUP)
            pltpu.make_async_copy(src.at[:, cut, :], dst.at[:, cut, :], in_sem.at[a, g]).start()

    tables = ((pair_hbm, pair_tab), (owner_hbm, owner_tab), (tile_hbm, tile_tab))
    for i, (src, dst) in enumerate(tables):
        pltpu.make_async_copy(src, dst, tab_sem.at[i]).start()

    barrier = pltpu.get_barrier_semaphore()

    def tell(target):
        pl.semaphore_signal(barrier, inc=1, device_id={"acq": target}, device_id_type=MESH)

    tell(left)
    tell(right)

    def say(r):
        for target in (me + 2**r, me + devices - 2**r):
            pl.semaphore_signal(
                ready.at[r], inc=1, device_id={"acq": wrap(target, devices)},
                device_id_type=MESH,
            )

    def hear(r):
        pl.semaphore_wait(ready.at[r], 2)

    def form_samples(g):
        for a, (src, dst) in enumerate(((amp_hbm, amp), (ph_hbm, ph))):
            cut = pl.ds(g * GROUP, GROUP)
            pltpu.make_async_copy(src.at[:, cut, :], dst.at[:, cut, :], in_sem.at[a, g]).wait()

        @pl.loop(0, LOOK)
        def _(i):
            cut = pl.ds(pl.multiple_of(g * GROUP + i * SUB, SUB), SUB)
            here = pl.ds(pl.multiple_of(i * SUB, SUB), SUB)
            for a in range(2):
                size = amp[a, cut, :]
                sin, cos = sincos(ph[a, cut, :])
                real, imag = size * cos, size * sin
                for lt in range(lane_tiles):
                    lanes = slice(lt * LANES, (lt + 1) * LANES)
                    smp[g, 2 * a, lt, here, :] = real[:, lanes]
                    smp[g, 2 * a + 1, lt, here, :] = imag[:, lanes]

    def sample_copy(side, k):
        if side == 0:
            return remote(smp.at[k], from_left.at[k], s_send.at[0, k], s_recv.at[0, k], right)
        return remote(smp.at[2 + k], from_right.at[k], s_send.at[1, k], s_recv.at[1, k], left)

    form_samples(0)
    form_samples(2)
    pl.semaphore_wait(barrier, 2)
    core = lax.axis_index("slab")
    say(0)

    @pl.when(core == 0)
    def _():
        sample_copy(0, 0).start()
        sample_copy(1, 0).start()

    form_samples(1)
    form_samples(3)

    @pl.when(core == 0)
    def _():
        sample_copy(0, 1).start()
        sample_copy(1, 1).start()

    @pl.when(core == 1)
    def _():
        sample_copy(0, 0).start()
        sample_copy(1, 0).start()

    hear(0)
    say(1)

    raw = lax.broadcasted_iota(jnp.int32, win.shape, 0)
    low = lax.broadcasted_iota(jnp.int32, win.shape, 1) * LOOK
    win[...] = jnp.where((raw >= low) & (raw < low + LOOK), 1.0, 0.0).astype(BF16)

    def look(count):
        x = acc[0:count, :]
        high = x.astype(BF16)
        rest = (x - high.astype(F32)).astype(BF16)
        return jnp.dot(high, win[...], preferred_element_type=F32) + jnp.dot(
            rest, win[...], preferred_element_type=F32
        )

    hear(1)
    say(2)

    for i, (src, dst) in enumerate(tables):
        pltpu.make_async_copy(src, dst, tab_sem.at[i]).wait()
    pair_ref, pair_sec = pair_tab[:, 0, :], pair_tab[:, 1, :]
    key = pair_ref * 256 + pair_sec
    base = 2 * me

    def key_of(i, j):
        return (base + i) * 256 + base + j

    codes = [[key_of(i - 2, j) for i in range(2) for j in range(2)],
             [key_of(i, j + 2) for i in range(2) for j in range(2)]]
    code_own = key_of(0, 1)

    def count_of(code):
        return total(jnp.where(key == code, 1.0, 0.0))

    weight = [[count_of(c) for c in side] for side in codes]
    weight_own = count_of(code_own)

    index = (
        lax.broadcasted_iota(jnp.int32, (4, LANES), 0) * LANES
        + lax.broadcasted_iota(jnp.int32, (4, LANES), 1)
    ).astype(F32)
    key_f = key.astype(F32)
    big = 1e6
    left_over = jnp.where(owner_tab[...] == me, index, big)
    slot_key = []
    for _ in range(4):
        first = smallest(left_over)
        hit = index == first
        slot_key.append(total(jnp.where(hit, key_f, 0.0)).astype(jnp.int32))
        left_over = jnp.where(hit, big, left_over)

    hear(2)
    say(3)

    ones = jnp.ones((LANES, LANES), BF16)
    window_dev = lax.rem(
        lax.broadcasted_iota(jnp.int32, (rows_w, LANES), 0)
        + (plane * columns + devices - HALO),
        devices,
    )
    for i in range(2):
        acq = 2 * window_dev + i
        hits = jnp.zeros((rows_w, LANES), F32)
        for member in (pair_ref, pair_sec):
            for q in range(4):
                hits = hits + jnp.where(acq == member[q : q + 1, :], 1.0, 0.0)
        deg[i] = 1.0 + jnp.dot(hits.astype(BF16), ones, preferred_element_type=F32)

    tile = lax.broadcasted_iota(jnp.int32, (SUB, LANES), 1).astype(F32)
    place = lax.broadcasted_iota(jnp.int32, (SUB, LANES), 0)
    holder = (place // TILE_CAP) * columns + cs
    free = jnp.where(tile_tab[...] == holder, tile, big)
    first = jnp.min(free, axis=1, keepdims=True)
    second = jnp.min(jnp.where(tile == first, big, free), axis=1, keepdims=True)
    wanted = jnp.where(lax.rem(place, TILE_CAP) == 0, first, second)
    pick[...] = jnp.where(tile == wanted, 1.0, 0.0)

    hear(3)
    say(4)

    @pl.when(core == 1)
    def _():
        sample_copy(0, 1).start()
        sample_copy(1, 1).start()

    @pl.loop(0, 4)
    def _(g):
        @pl.loop(0, lane_tiles)
        def _(lt):
            lanes = pl.ds(pl.multiple_of(lt * LANES, LANES), LANES)
            sums = [jnp.zeros((SUB, LANES), F32) for _ in range(4)]
            for kk in range(LOOK):
                x = [smp[g, f, lt, pl.ds(kk, SUB, stride=LOOK), :] for f in range(4)]
                sums[0] = sums[0] + (x[0] * x[0] + x[1] * x[1])
                sums[1] = sums[1] + (x[2] * x[2] + x[3] * x[3])
                sums[2] = sums[2] + (x[0] * x[2] + x[1] * x[3])
                sums[3] = sums[3] + (x[1] * x[2] - x[0] * x[3])
            for f in range(4):
                acc[f * SUB : (f + 1) * SUB, lanes] = sums[f]

        out = look(4 * SUB)
        cut = pl.ds(pl.multiple_of(g * SUB, SUB), SUB)
        power_ref, power_sec = out[0:SUB], out[SUB : 2 * SUB]
        power[0, cut, :] = power_ref
        power[1, cut, :] = power_sec
        scale = 1.0 / jnp.sqrt(power_ref * power_sec)
        loc[0, cut, :] = out[2 * SUB : 3 * SUB] * scale
        loc[1, cut, :] = out[3 * SUB : 4 * SUB] * scale

    for f in range(2):
        for g in range(columns // SUB):
            emsg[pl.ds(SLOT * SUB * g + 8 + f, SUB, stride=SLOT), :] = (
                loc[f, SUB * g : SUB * (g + 1), :] * weight_own
            )

    hear(4)
    say(5)

    vec[...] = jnp.zeros_like(vec)
    vec[0, 0] = jnp.ones(vec.shape[2:], F32)
    vec[0, 2] = jnp.ones(vec.shape[2:], F32)
    for f in range(8):
        edge[f, 0:SUB, :] = jnp.zeros((SUB, LANES), F32)
    ebuf[0:SLOT, :] = jnp.zeros((SLOT, LANES), F32)

    def gee_copy(side, k):
        if side == 0:
            part = gee.at[0, :, pl.ds(SUB * k, SUB), :]
            return remote(
                part, gee.at[1, :, pl.ds(SUB * k, SUB), :], g_send.at[0, k], g_recv.at[0, k], left
            )
        part = gee.at[1, :, pl.ds(half + SUB * k, SUB), :]
        return remote(
            part, gee.at[0, :, pl.ds(half + SUB * k, SUB), :],
            g_send.at[1, k], g_recv.at[1, k], right,
        )

    def slot_rows(slot):
        return pl.ds(pl.multiple_of(SLOT * slot, SLOT), ROWS)

    def window_rows(slot):
        return slot_rows(slot + 1)

    hear(5)


    for k in range(2):
        for side in range(2):
            sample_copy(side, k).wait_recv()
            other = (from_left, from_right)[side]
            first_col = side * half + k * SUB

            @pl.loop(0, lane_tiles)
            def _(lt):
                lanes = pl.ds(pl.multiple_of(lt * LANES, LANES), LANES)
                sums = [jnp.zeros((SUB, LANES), F32) for _ in range(10)]
                for kk in range(LOOK):
                    cut = pl.ds(kk, SUB, stride=LOOK)
                    near = [smp[2 * side + k, f, lt, cut, :] for f in range(4)]
                    far = [other[k, f, lt, cut, :] for f in range(4)]
                    ref, sec = (far, near) if side == 0 else (near, far)
                    for i in range(2):
                        for j in range(2):
                            f = (2 * i + j) * 2
                            sums[f] = sums[f] + (
                                ref[2 * i] * sec[2 * j] + ref[2 * i + 1] * sec[2 * j + 1]
                            )
                            sums[f + 1] = sums[f + 1] + (
                                ref[2 * i + 1] * sec[2 * j] - ref[2 * i] * sec[2 * j + 1]
                            )
                        sums[8 + i] = sums[8 + i] + (
                            far[2 * i] * far[2 * i] + far[2 * i + 1] * far[2 * i + 1]
                        )
                for f in range(10):
                    acc[f * SUB : (f + 1) * SUB, lanes] = sums[f]

            out = look(10 * SUB)
            for i in range(2):
                for j in range(2):
                    mine, theirs = (j, i) if side == 0 else (i, j)
                    scale = 1.0 / jnp.sqrt(
                        power[mine, first_col : first_col + SUB, :]
                        * out[(8 + theirs) * SUB : (9 + theirs) * SUB]
                    )
                    for part in range(2):
                        f = (2 * i + j) * 2 + part
                        value = out[f * SUB : (f + 1) * SUB] * scale
                        gee[side, f, first_col : first_col + SUB, :] = value
                        emsg[pl.ds(SLOT * first_col + f, SUB, stride=SLOT), :] = (
                            value * weight[side][2 * i + j]
                        )

            edge_at = cs - 1 if side == 0 else cs

            @pl.loop(0, SUB)
            def _(i):
                c = first_col + wrap(cs + i, SUB)
                src = emsg.at[slot_rows(c), :]

                @pl.when(edge_at < HALO)
                def _():
                    remote(
                        src, ebuf.at[window_rows(columns + HALO + edge_at), :], h_send, e_recv,
                        below + c,
                    ).start()

                @pl.when(edge_at >= columns - HALO)
                def _():
                    remote(
                        src, ebuf.at[window_rows(edge_at - (columns - HALO)), :], h_send, e_recv,
                        above + c,
                    ).start()

                @pl.when(c != cs)
                def _():
                    remote(
                        src, ebuf.at[window_rows(HALO + edge_at), :], e_send, e_recv,
                        first_of_plane + c,
                    ).start()

        for side in range(2):
            gee_copy(side, k).start()

    shift = (cs < half).astype(jnp.int32)
    ebuf[window_rows(HALO + cs - shift), :] = emsg[slot_rows(cs), :]

    await_bytes(ebuf.at[pl.ds(0, (rows_w - 1) * ROWS), :], e_recv)
    for f in range(ROWS):
        back_by = shift if f >= 8 else 0
        for t in range(rows_w // SUB):
            edge[f, SUB * (t + 1) : SUB * (t + 2), :] = ebuf[
                pl.ds(f + SLOT * (SUB * t + 1 - back_by), SUB, stride=SLOT), :
            ]

    def step(t, kappa):
        now = lax.rem(t, 2)
        size = jnp.zeros((SUB, LANES), F32)
        for w in range(rows_w // SUB):
            cut = slice(SUB * w, SUB * (w + 1))
            mid = slice(SUB * (w + 1), SUB * (w + 2))
            low = slice(SUB * (w + 1) - 1, SUB * (w + 2) - 1)
            high = slice(SUB * (w + 1) + 1, SUB * (w + 2) + 1)
            u = [vec[now, f, mid, :] for f in range(4)]
            u_low = [vec[now, f, low, :] for f in range(4)]
            u_high = [vec[now, f, high, :] for f in range(4)]
            lr, li = edge[8, mid, :], edge[9, mid, :]
            for a in range(2):
                d = deg[a, cut, :]
                o = 1 - a
                sign = 1.0 if a == 0 else -1.0
                re = d * u[2 * a] + lr * u[2 * o] - sign * (li * u[2 * o + 1])
                im = d * u[2 * a + 1] + lr * u[2 * o + 1] + sign * (li * u[2 * o])
                for b in range(2):
                    f = (2 * a + b) * 2
                    gr, gi = edge[f, mid, :], edge[f + 1, mid, :]
                    re = re + (gr * u_high[2 * b] - gi * u_high[2 * b + 1])
                    im = im + (gr * u_high[2 * b + 1] + gi * u_high[2 * b])
                    f = (2 * b + a) * 2
                    gr, gi = edge[f, low, :], edge[f + 1, low, :]
                    re = re + (gr * u_low[2 * b] + gi * u_low[2 * b + 1])
                    im = im + (gr * u_low[2 * b + 1] - gi * u_low[2 * b])
                vec[1 - now, 2 * a, mid, :] = re
                vec[1 - now, 2 * a + 1, mid, :] = im
                if HALO // SUB <= w < (HALO + columns) // SUB:
                    size = size + (re * re + im * im)
        return (jnp.sum(size, axis=0, keepdims=True) + EPS * kappa) / acq_total

    kappa = lax.fori_loop(0, ITERS, step, jnp.full((1, LANES), 1.0 / planes, F32))
    last = ITERS % 2
    qual = jnp.zeros((SUB, LANES), F32)
    for w in range(HALO // SUB, (HALO + columns) // SUB):
        mid = slice(SUB * (w + 1), SUB * (w + 2))
        high = slice(SUB * (w + 1) + 1, SUB * (w + 2) + 1)
        u = [vec[last, f, mid, :] for f in range(4)]
        u_high = [vec[last, f, high, :] for f in range(4)]
        qual = qual + edge[8, mid, :] * (u[0] * u[2] + u[1] * u[3])
        qual = qual - edge[9, mid, :] * (u[0] * u[3] - u[1] * u[2])
        for a in range(2):
            for b in range(2):
                f = (2 * a + b) * 2
                ur, ui = u[2 * a], u[2 * a + 1]
                vr, vi = u_high[2 * b], u_high[2 * b + 1]
                qual = qual + edge[f, mid, :] * (ur * vr + ui * vi)
                qual = qual - edge[f + 1, mid, :] * (ur * vi - ui * vr)
    nmsg[0:1, :] = kappa
    nmsg[1:2, :] = jnp.sum(qual, axis=0, keepdims=True)

    for i in range(1, planes):
        target = wrap(me + i * columns, devices)
        remote(nmsg, nbuf.at[plane], n_send, n_recv, target).start()
    nbuf[plane] = nmsg[...]
    await_bytes(nbuf.at[pl.ds(0, planes - 1)], n_recv)
    both = nbuf[0]
    for i in range(1, planes):
        both = both + nbuf[i]
    kappa, qual = both[0:1, :], both[1:2, :]
    alpha = 1.0 / jnp.sqrt(kappa)
    qual = qual / (kappa * pairs_total)

    for g in range(columns // SUB):
        cut = slice(SUB + HALO + SUB * g, SUB + HALO + SUB * (g + 1))
        for f in range(4):
            umsg[pl.ds(SUB * SUB * g + f, SUB, stride=SUB), :] = vec[last, f, cut, :] * alpha
        umsg[pl.ds(SUB * SUB * g + 4, SUB, stride=SUB), :] = jnp.broadcast_to(qual, (SUB, LANES))

    def back_rows(slot):
        return pl.ds(pl.multiple_of(SUB * slot, SUB), BACK)

    @pl.loop(1, columns)
    def _(i):
        c = wrap(cs + i, columns)
        remote(
            umsg.at[back_rows(c), :], ubuf.at[back_rows(cs), :], u_send, u_recv,
            first_of_plane + c,
        ).start()

    ubuf[back_rows(cs), :] = umsg[back_rows(cs), :]

    for side in range(2):
        for k in range(2):
            gee_copy(side, k).wait_recv()
    for slot in range(4):
        hit_own = slot_key[slot] == code_own
        hits = [[slot_key[slot] == c for c in side] for side in codes]

        @pl.loop(0, columns // SUB)
        def _(g):
            cut = pl.ds(pl.multiple_of(g * SUB, SUB), SUB)
            for part in range(2):
                value = jnp.where(hit_own, loc[part, cut, :], 0.0)
                for side in range(2):
                    for c in range(4):
                        value = jnp.where(hits[side][c], gee[side, 2 * c + part, cut, :], value)
                ifg_ref[slot, part, cut, :] = value

    def back(f, g):
        return ubuf[pl.ds(SUB * SUB * g + f, SUB, stride=SUB), :]

    await_bytes(ubuf.at[pl.ds(0, (columns - 1) * BACK), :], u_recv)
    for g in range(columns // SUB):
        cut = slice(SUB * g, SUB * (g + 1))
        for f in range(4):
            link_ref[f // 2, f % 2, cut, :] = back(f, g)
    quality = jnp.concatenate([back(4, g) for g in range(columns // SUB)], axis=0)
    chosen[...] = lax.dot_general(
        pick[...], quality, (((1,), (1,)), ((), ())),
        precision=lax.Precision.HIGHEST, preferred_element_type=F32,
    )
    for a in range(TILE_CAP):
        qual_ref[a] = chosen[pl.ds(plane * TILE_CAP + a, 1), :]

    for side in range(2):
        for k in range(2):
            sample_copy(side, k).wait_send()
            gee_copy(side, k).wait_send()
    await_bytes(emsg.at[pl.ds(0, (columns - 1) * ROWS), :], e_send)
    await_bytes(ubuf.at[pl.ds(0, (columns - 1) * BACK), :], u_send)
    await_bytes(nbuf.at[pl.ds(0, planes - 1)], n_send)

    for side in range(2):
        edge_at = cs - 1 if side == 0 else cs

        @pl.when(jnp.logical_or(edge_at < HALO, edge_at >= columns - HALO))
        def _():
            await_bytes(emsg.at[pl.ds(0, half * ROWS), :], h_send)


def write_out(ifg_in, link_in, qual_in, ifg_out, link_out, qual_out, sem):
    copies = [
        pltpu.make_async_copy(src, dst, sem.at[i])
        for i, (src, dst) in enumerate(
            ((ifg_in, ifg_out), (link_in, link_out), (qual_in, qual_out))
        )
    ]
    for copy in copies:
        copy.start()
    for copy in copies:
        copy.wait()


def per_device(slc_amplitude, slc_phase, pair_list, pair_owner, tile_map):
    columns = slc_amplitude.shape[1] // LOOK
    raw = slc_amplitude.shape[2]
    pairs = pair_list.reshape(-1, LANES, 2).transpose(0, 2, 1)
    owners = pair_owner.reshape(-1, LANES)
    tiles = tile_map.reshape(-1, LANES)
    hbm = pl.BlockSpec(memory_space=pltpu.HBM)
    rows_w = columns + 2 * HALO
    planes = lax.axis_size("acq") // columns
    dma = pltpu.SemaphoreType.DMA
    vmem = pl.BlockSpec(memory_space=pltpu.VMEM)
    arguments = (slc_amplitude, slc_phase, pairs, owners, tiles)
    results = pl.pallas_call(
        kernel,
        name="phase_linking",
        out_shape=(
            jax.ShapeDtypeStruct((4, 2, columns, LANES), F32),
            jax.ShapeDtypeStruct((2, 2, columns, LANES), F32),
            jax.ShapeDtypeStruct((TILE_CAP, 1, columns), F32),
        ),
        in_specs=[hbm] * 5,
        out_specs=(vmem, vmem, vmem),
        scratch_shapes=[
            pltpu.VMEM(slc_amplitude.shape, F32),
            pltpu.VMEM(slc_amplitude.shape, F32),
            pltpu.VMEM(pairs.shape, jnp.int32),
            pltpu.VMEM(owners.shape, jnp.int32),
            pltpu.VMEM(tiles.shape, jnp.int32),
            pltpu.VMEM((4, 4, raw // LANES, GROUP, LANES), F32),
            pltpu.VMEM((2, 4, raw // LANES, GROUP, LANES), F32),
            pltpu.VMEM((2, 4, raw // LANES, GROUP, LANES), F32),
            pltpu.VMEM((10 * SUB, raw), F32),
            pltpu.VMEM((raw, LANES), BF16),
            pltpu.VMEM((2, 8, columns, LANES), F32),
            pltpu.VMEM((2, columns, LANES), F32),
            pltpu.VMEM((2, columns, LANES), F32),
            pltpu.VMEM((columns * SLOT, LANES), F32),
            pltpu.VMEM(((rows_w + 1) * SLOT, LANES), F32),
            pltpu.VMEM((10, rows_w + 2 * SUB, LANES), F32),
            pltpu.VMEM((2, 4, rows_w + 2 * SUB, LANES), F32),
            pltpu.VMEM((2, rows_w, LANES), F32),
            pltpu.VMEM((columns * SUB, LANES), F32),
            pltpu.VMEM((columns * SUB, LANES), F32),
            pltpu.VMEM((2, LANES), F32),
            pltpu.VMEM((planes, 2, LANES), F32),
            pltpu.VMEM((SUB, LANES), F32),
            pltpu.VMEM((SUB, columns), F32),
            dma((2, 4)), dma((3,)), dma((2, 2)), dma((2, 2)), dma((2, 2)), dma((2, 2)),
            pltpu.SemaphoreType.REGULAR((6,)), dma, dma, dma, dma, dma, dma, dma,
        ],
        compiler_params=pltpu.CompilerParams(
            collective_id=0, has_side_effects=True, vmem_limit_bytes=40 * 2**20
        ),
    )(*[pltpu.with_memory_space_constraint(x, pltpu.HBM) for x in arguments])
    return pl.pallas_call(
        write_out,
        name="write_out",
        out_shape=[jax.ShapeDtypeStruct(x.shape, F32) for x in results],
        in_specs=[vmem] * 3,
        out_specs=[hbm] * 3,
        scratch_shapes=[dma((3,))],
        compiler_params=pltpu.CompilerParams(vmem_limit_bytes=2**20),
    )(*results)


def solution(mesh):
    in_specs = (P("acq", None, "slab"), P("acq", None, "slab"), P(), P(), P())
    out_specs = (P("acq", None, None, "slab"), P("acq", None, None, "slab"), P("acq", "slab", None))
    return jax.shard_map(
        per_device, mesh=mesh, in_specs=in_specs, out_specs=out_specs, check_vma=False
    )
```
